256 devices in a mesh: section: 4 (over x), dp: 64 (over y, z, core).
Axes of the slice: x: 4, y: 4, z: 8, core: 2. Of those that a mesh axis runs over, the one named last changes fastest.
Arguments:
- clean_latent: bfloat16 [8192, 1536], P('dp'), may hold values from -60 to 60
- noise_latent: bfloat16 [8192, 1536], P('dp'), may hold values from -6 to 6
- teacher_velocity: bfloat16 [8192, 1536], P('dp'), may hold values from -6 to 6
- step_index: int32 [8192], P('dp'), may hold values from 0 to 3
- modulation: float32 [4, 4, 1536], P('section'), may hold values from -0.6 to 0.6
- up_weight: bfloat16 [4, 36864, 128], P('section', 'dp'), may hold values from -0.21875 to 0.21875
- up_rows: int32 [4, 48, 6], P('section'), may hold values from 0 to 11, as said below
- down_weight: bfloat16 [4, 36864, 128], P('section'), may hold values from -0.109375 to 0.109375
- down_rows: int32 [4, 12, 24], P('section'), may hold values from 0 to 47, as said below
Outputs:
- grad_down: float32 [4, 36864, 128], P('section', 'dp')
The draws below stay inside these ranges and needn't reach their ends.
Inputs may be any that keep to these rules, and one draw needn't show every extreme that they name: For every section s and hidden block c, up_rows[s, c] holds 6 different feature blocks. For every section s and feature block e, down_rows[s, e] holds 24 different hidden blocks.
All inputs are finite; a program needn't handle non-finite values.
Results may differ from the reference program's by a relative error of at most 0.004.
Values may be sent and summed in bfloat16 or wider, within the bound.
No kernel may reach another device: no remote copies, remote signals or barrier semaphores. Data moves between devices by JAX's collectives and lax.ppermute only.
A program may use at most 128 MiB of HBM per device.

```python
import math
import jax
import jax.numpy as jnp
from jax import lax

WIDTH = 1536
BLOCK = 128
STEPS = 4
SECTIONS = 4
WIDTH_BLOCKS = 12
HIDDEN_BLOCKS = 48
KEEP_UP = 6
KEEP_DOWN = 24
TOKENS = 8192


def draw_clean_latent(key, part):
    first = jax.random.fold_in(key, 0)
    base = jnp.clip(jax.random.normal(first, (TOKENS, WIDTH), jnp.float32), -5.0, 5.0)
    return base.astype(jnp.bfloat16)


def pattern(key, section_count, columns, choices, keep):
    keys = jax.random.split(key, section_count * columns + 1)
    perms = jax.vmap(lambda subkey: jax.random.permutation(subkey, choices))(keys[:-1]).reshape(section_count, columns, choices)
    pick_first = jax.random.randint(keys[-1], (section_count, 1, 1), 0, columns)
    pick_second = (pick_first + 1) % columns
    positions = jnp.arange(choices, dtype=jnp.int32)[None, None, :]

    def front(value):
        return jnp.where(positions == 0, value, jnp.where(perms == value, perms[:, :, :1], perms))
    column_ids = jnp.arange(columns, dtype=jnp.int32)[None, :, None]
    arranged = jnp.where(column_ids == pick_first, front(0), jnp.where(column_ids == pick_second, front(choices - 1), perms))
    return arranged[:, :, :keep].astype(jnp.int32)


def draw_up_rows(key, part):
    return pattern(jax.random.fold_in(key, 11), SECTIONS, HIDDEN_BLOCKS, WIDTH_BLOCKS, KEEP_UP)


def draw_down_rows(key, part):
    return pattern(jax.random.fold_in(key, 23), SECTIONS, WIDTH_BLOCKS, HIDDEN_BLOCKS, KEEP_DOWN)


def plant(array, rng, smallest, top_value):
    place = [jax.random.randint(jax.random.fold_in(rng, axis), (), 0, length) for axis, length in enumerate(array.shape)]
    widest = array.shape.index(max(array.shape))
    neighbour = place[:widest] + [(place[widest] + 1) % array.shape[widest]] + place[widest + 1:]
    return array.at[tuple(place)].set(smallest).at[tuple(neighbour)].set(top_value)


def block_levels(key, shape, cuts, least, high):
    loudness = 1.0
    for dim, shards_of in cuts:
        heights = jax.random.uniform(jax.random.fold_in(jax.random.fold_in(key, 6), dim), (shards_of,), jnp.float32, least / len(cuts), high / len(cuts))
        loudness = loudness * jnp.repeat(jnp.exp(heights), shape[dim] // shards_of).reshape((-1,) + (1,) * (len(shape) - 1 - dim))
    return loudness


def normal_values(own_key, shape, scale, reach, shards=(), held_as=jnp.bfloat16):
    values = jax.random.normal(own_key, shape, jnp.float32) * scale
    if len(shards) > 0:
        values = block_levels(own_key, shape, shards, -0.22, 0.18) * values
    return jnp.clip(values, min=-reach, max=reach).astype(held_as)


def setup_inputs(seed: int = 0) -> dict:
    streams_of = jax.random.split(jax.random.key(seed), 10)
    return {
        "clean_latent": draw_clean_latent(jax.random.fold_in(streams_of[9], 71), 0),
        "noise_latent": normal_values(streams_of[1], (TOKENS, WIDTH), 1.0, 6.0, ((0, 64),)),
        "teacher_velocity": normal_values(streams_of[2], (TOKENS, WIDTH), 1.0, 6.0, ((0, 64),)),
        "step_index": plant(jax.random.randint(streams_of[3], (TOKENS,), 0, STEPS), jax.random.fold_in(streams_of[3], 1), 0, STEPS - 1).astype(jnp.int32),
        "modulation": jnp.clip(jax.random.uniform(streams_of[4], (SECTIONS, STEPS, WIDTH), jnp.float32, -0.6, 0.6) * block_levels(streams_of[4], (SECTIONS, STEPS, WIDTH), ((0, 4),), -0.4, 0.0), -0.6, 0.6),
        "up_weight": normal_values(streams_of[5], (SECTIONS, HIDDEN_BLOCKS * KEEP_UP * BLOCK, BLOCK), (KEEP_UP * BLOCK) ** -0.5, 0.21875, ((0, 4), (1, 64))),
        "up_rows": draw_up_rows(jax.random.fold_in(streams_of[9], 71), 0),
        "down_weight": normal_values(streams_of[7], (SECTIONS, WIDTH_BLOCKS * KEEP_DOWN * BLOCK, BLOCK), (KEEP_DOWN * BLOCK) ** -0.5, 0.109375, ((0, 4),)),
        "down_rows": draw_down_rows(jax.random.fold_in(streams_of[9], 71), 0),
    }


EPSILON = 1e-06
HIGHEST_PRECISION = lax.Precision.HIGHEST

def product(form, left, right):
    return jnp.einsum(form, left.astype(jnp.float32), right.astype(jnp.float32), precision=HIGHEST_PRECISION)

def activation(values):
    return jax.nn.gelu(values, approximate=True)

def lookup(step_values, table):
    onehot = (step_values[:, None] == jnp.arange(table.shape[0], dtype=jnp.int32)[None, :]).astype(jnp.float32)
    return lax.optimization_barrier(jnp.sum(onehot[:, :, None] * table[None, :, :], axis=1))

def section_forward(stream, scale_rows, up_blocks, up_index, down_blocks, down_index):
    row_count, feature_count = stream.shape
    block_size = up_blocks.shape[-1]
    stream_wide = stream.astype(jnp.float32)
    inverse = lax.rsqrt(lax.optimization_barrier(jnp.mean(stream_wide * stream_wide, axis=-1, keepdims=True)) + EPSILON)
    normed = (stream_wide * inverse * (1.0 + scale_rows)).astype(jnp.bfloat16)
    picked = normed.reshape(row_count, feature_count // block_size, block_size)[:, up_index, :]
    preact = product('rcki,ckij->rcj', picked, up_blocks)
    hidden = activation(preact).astype(jnp.bfloat16)
    gathered = hidden[:, down_index, :]
    mixed_out = product('rekj,ekjf->ref', gathered, down_blocks)
    result = (stream_wide + mixed_out.reshape(row_count, feature_count)).astype(jnp.bfloat16)
    return (result, preact.reshape(row_count, -1), hidden.reshape(row_count, -1))

def section_backward(cotangent, stream, scale_rows, preact, up_blocks, up_index, down_blocks, down_index):
    row_count, feature_count = stream.shape
    block_size = up_blocks.shape[-1]
    hidden_count = preact.shape[1]
    grad_blocks = cotangent.reshape(row_count, feature_count // block_size, block_size)
    grad_gathered = product('ref,ekjf->rekj', grad_blocks, down_blocks)
    grad_hidden = jnp.zeros((row_count, hidden_count // block_size, block_size), jnp.float32).at[:, down_index, :].add(grad_gathered)
    activated, pullback = jax.vjp(activation, preact.reshape(row_count, hidden_count // block_size, block_size))
    grad_preact = pullback(grad_hidden)[0].astype(jnp.bfloat16)
    grad_picked = product('rcj,ckij->rcki', grad_preact, up_blocks)
    grad_normed = jnp.zeros((row_count, feature_count // block_size, block_size), jnp.float32).at[:, up_index, :].add(grad_picked)
    grad_normed = grad_normed.reshape(row_count, feature_count)
    stream_wide = stream.astype(jnp.float32)
    inverse = lax.rsqrt(lax.optimization_barrier(jnp.mean(stream_wide * stream_wide, axis=-1, keepdims=True)) + EPSILON)
    scaled = grad_normed * (1.0 + scale_rows)
    grad_stream = inverse * scaled - stream_wide * inverse * inverse * inverse * lax.optimization_barrier(jnp.mean(scaled * stream_wide, axis=-1, keepdims=True))
    return (cotangent.astype(jnp.float32) + grad_stream).astype(jnp.bfloat16)

def weight_term(hidden, cotangent, down_index, block_size):
    row_count = hidden.shape[0]
    gathered = hidden.reshape(row_count, -1, block_size)[:, down_index, :]
    return product('tejh,tef->ejhf', gathered, cotangent.reshape(row_count, -1, block_size))

def reference(clean_latent, noise_latent, teacher_velocity, step_index, modulation, up_weight, up_rows, down_weight, down_rows):
    blocks_up = up_weight.reshape(SECTIONS, HIDDEN_BLOCKS, KEEP_UP, BLOCK, BLOCK)
    blocks_down = down_weight.reshape(SECTIONS, WIDTH_BLOCKS, KEEP_DOWN, BLOCK, BLOCK)
    row_block = math.gcd(TOKENS, 512)
    block_count = TOKENS // row_block
    loss_scale = 1.0 / math.sqrt(TOKENS)

    def one_block(running, pieces):
        clean_rows, noise_rows, target_rows, step_values = pieces
        fraction = (step_values.astype(jnp.float32) + 1.0) / STEPS
        stream = ((1.0 - fraction)[:, None] * clean_rows.astype(jnp.float32) + fraction[:, None] * noise_rows.astype(jnp.float32)).astype(jnp.bfloat16)
        kept_values = []
        for section_number in range(SECTIONS):
            scale_rows = lookup(step_values, modulation[section_number])
            stream_in = stream
            stream, preact, hidden = section_forward(stream_in, scale_rows, blocks_up[section_number], up_rows[section_number], blocks_down[section_number], down_rows[section_number])
            kept_values.append((stream_in, scale_rows, preact, hidden))
        cotangent = ((stream.astype(jnp.float32) - target_rows.astype(jnp.float32)) * loss_scale).astype(jnp.bfloat16)
        weight_terms = [None] * SECTIONS
        for section_number in reversed(range(SECTIONS)):
            stream_in, scale_rows, preact, hidden = kept_values[section_number]
            weight_terms[section_number] = weight_term(hidden, cotangent, down_rows[section_number], BLOCK)
            cotangent = section_backward(cotangent, stream_in, scale_rows, preact, blocks_up[section_number], up_rows[section_number], blocks_down[section_number], down_rows[section_number])
        return (running + jnp.stack(weight_terms), None)
    initial = jnp.zeros((SECTIONS, WIDTH_BLOCKS, KEEP_DOWN, BLOCK, BLOCK), jnp.float32)
    pieces = (clean_latent.reshape(block_count, row_block, WIDTH), noise_latent.reshape(block_count, row_block, WIDTH), teacher_velocity.reshape(block_count, row_block, WIDTH), step_index.reshape(block_count, row_block))
    running, unused = lax.scan(one_block, initial, pieces)
    return running.reshape(SECTIONS, WIDTH_BLOCKS * KEEP_DOWN * BLOCK, BLOCK)
```

```python
import math

import jax
import jax.numpy as jnp
from jax import lax
from jax.experimental import pallas as pl
from jax.experimental.pallas import tpu as pltpu
from jax.sharding import PartitionSpec as P

EPSILON = 1e-06
F32 = jnp.float32
BF16 = jnp.bfloat16
STEPS_EACH = 4
GELU_A = math.sqrt(2.0 / math.pi)
GELU_B = 0.044715


def lane_block(index, size):
    return pl.ds(pl.multiple_of(index * size, size), size)


def split_range(total, parts):
    assert total % parts == 0
    return total // parts


def gelu_parts(v):
    squared = v * v
    t = jnp.tanh(v * (GELU_A + (GELU_A * GELU_B) * squared))
    half = 0.5 * (1.0 + t)
    slope = half + (0.5 * v) * (1.0 - t * t) * (GELU_A + (3.0 * GELU_A * GELU_B) * squared)
    return v * half, slope


def forward_kernel(
    keep_up, keep_down, up_per, down_per, full, up_index, down_index, x_ref, s_ref, uw_ref, dw_ref, *rest
):
    if full:
        out_ref, slope_ref, hidden_out_ref, normed, hidden = rest
    else:
        out_ref, normed, hidden = rest
    size = normed.shape[-1]
    width_blocks = normed.shape[0]
    step = pl.program_id(0)

    @pl.when(step == 0)
    def _():
        x = x_ref[...].astype(F32)
        inverse = lax.rsqrt(jnp.mean(x * x, axis=-1, keepdims=True) + EPSILON)
        for b in range(width_blocks):
            cols = slice(b * size, (b + 1) * size)
            piece = x_ref[:, cols].astype(F32)
            normed[b] = (piece * inverse * s_ref[:, cols]).astype(BF16)

    @pl.when(step < STEPS_EACH)
    def _():
        for cc in range(up_per):
            c = step * up_per + cc
            left = jnp.concatenate(
                [normed[up_index[c * keep_up + k]] for k in range(keep_up)], axis=1
            )
            rows = keep_up * size
            pre = jnp.dot(left, uw_ref[cc * rows : (cc + 1) * rows, :], preferred_element_type=F32)
            act, slope = gelu_parts(pre)
            act = act.astype(BF16)
            hidden[c] = act
            if full:
                slope_ref[cc] = slope
                hidden_out_ref[cc] = act

    @pl.when(step >= STEPS_EACH)
    def _():
        group = 4
        for ee in range(down_per):
            e = (step - STEPS_EACH) * down_per + ee
            total = x_ref[:, lane_block(e, size)].astype(F32)
            acc = None
            for k in range(0, keep_down, group):
                left = jnp.concatenate(
                    [hidden[down_index[e * keep_down + k + q]] for q in range(group)], axis=1
                )
                first = (ee * keep_down + k) * size
                term = jnp.dot(
                    left, dw_ref[first : first + group * size, :], preferred_element_type=F32
                )
                acc = term if acc is None else acc + term
            out_ref[:, lane_block(e, size)] = (total + acc).astype(BF16)


def first_half(i, *_):
    return (jnp.minimum(i, STEPS_EACH - 1), 0)


def second_half(i, *_):
    return (jnp.maximum(i - STEPS_EACH, 0), 0)


def whole(i, *_):
    return (0, 0)


def section_forward(stream, scale_plus, up_flat, up_index, down_flat, down_index, full):
    rows, features = stream.shape
    size = up_flat.shape[1]
    hidden_blocks, keep_up = up_index.shape
    width_blocks, keep_down = down_index.shape
    up_per = split_range(hidden_blocks, STEPS_EACH)
    down_per = split_range(width_blocks, STEPS_EACH)
    out_shape = [jax.ShapeDtypeStruct((rows, features), BF16)]
    out_specs = [pl.BlockSpec((rows, features), whole)]
    if full:
        part = lambda i, *_: (jnp.minimum(i, STEPS_EACH - 1), 0, 0)
        out_shape += [
            jax.ShapeDtypeStruct((hidden_blocks, rows, size), F32),
            jax.ShapeDtypeStruct((hidden_blocks, rows, size), BF16),
        ]
        out_specs += [pl.BlockSpec((up_per, rows, size), part)] * 2

    def body(*refs):
        forward_kernel(keep_up, keep_down, up_per, down_per, full, *refs)

    return pl.pallas_call(
        body,
        out_shape=out_shape,
        grid_spec=pltpu.PrefetchScalarGridSpec(
            num_scalar_prefetch=2,
            grid=(2 * STEPS_EACH,),
            in_specs=[
                pl.BlockSpec((rows, features), whole),
                pl.BlockSpec((rows, features), whole),
                pl.BlockSpec((up_flat.shape[0] // STEPS_EACH, size), first_half),
                pl.BlockSpec((down_flat.shape[0] // STEPS_EACH, size), second_half),
            ],
            out_specs=out_specs,
            scratch_shapes=[
                pltpu.VMEM((width_blocks, rows, size), BF16),
                pltpu.VMEM((hidden_blocks, rows, size), BF16),
            ],
        ),
        compiler_params=pltpu.CompilerParams(
            dimension_semantics=("arbitrary",), vmem_limit_bytes=36 << 20
        ),
        cost_estimate=pl.CostEstimate(
            flops=4 * rows * up_flat.size, bytes_accessed=4 * up_flat.size, transcendentals=0
        ),
        name="forward_full" if full else "forward",
    )(up_index.reshape(-1), down_index.reshape(-1), stream, scale_plus, up_flat, down_flat)


def contract_last(left, right):
    return lax.dot_general(left, right, (((1,), (1,)), ((), ())), preferred_element_type=F32)


def backward_kernel(
    keep_up, keep_down, up_per, down_per, up_index, down_index,
    cot_ref, x_ref, s_ref, slope_ref, uw_ref, dw_ref, out_ref, grad_hidden, grad_normed,
):
    size = grad_hidden.shape[-1]
    width_blocks = grad_normed.shape[0]
    step = pl.program_id(0)

    @pl.when(step == 0)
    def _():
        grad_hidden[...] = jnp.zeros_like(grad_hidden)
        grad_normed[...] = jnp.zeros_like(grad_normed)

    @pl.when(step < STEPS_EACH)
    def _():
        group = 4
        for ee in range(down_per):
            e = step * down_per + ee
            left = cot_ref[:, lane_block(e, size)]
            for k in range(0, keep_down, group):
                first = (ee * keep_down + k) * size
                term = contract_last(left, dw_ref[first : first + group * size, :])
                for q in range(group):
                    h = down_index[e * keep_down + k + q]
                    grad_hidden[h] += term[:, q * size : (q + 1) * size]

    @pl.when(step >= STEPS_EACH)
    def _():
        group = 3
        for cc in range(up_per):
            c = (step - STEPS_EACH) * up_per + cc
            left = (slope_ref[cc] * grad_hidden[c]).astype(BF16)
            for k in range(0, keep_up, group):
                first = (cc * keep_up + k) * size
                term = contract_last(left, uw_ref[first : first + group * size, :])
                for q in range(group):
                    w = up_index[c * keep_up + k + q]
                    grad_normed[w] += term[:, q * size : (q + 1) * size]

    @pl.when(step == 2 * STEPS_EACH - 1)
    def _():
        x = x_ref[...].astype(F32)
        features = x.shape[1]
        inverse = lax.rsqrt(jnp.mean(x * x, axis=-1, keepdims=True) + EPSILON)
        along = jnp.zeros((x.shape[0], size), F32)
        for b in range(width_blocks):
            cols = slice(b * size, (b + 1) * size)
            scaled = grad_normed[b] * s_ref[:, cols]
            grad_normed[b] = scaled
            along += scaled * x_ref[:, cols].astype(F32)
        mean = jnp.sum(along, axis=-1, keepdims=True) * (1.0 / features)
        factor = inverse * inverse * inverse * mean
        for b in range(width_blocks):
            cols = slice(b * size, (b + 1) * size)
            grad = inverse * grad_normed[b] - x_ref[:, cols].astype(F32) * factor
            out_ref[:, cols] = (cot_ref[:, cols].astype(F32) + grad).astype(BF16)


def section_backward(cot, stream, scale_plus, slope, up_flat, up_index, down_flat, down_index):
    rows, features = stream.shape
    size = up_flat.shape[1]
    hidden_blocks, keep_up = up_index.shape
    width_blocks, keep_down = down_index.shape
    up_per = split_range(hidden_blocks, STEPS_EACH)
    down_per = split_range(width_blocks, STEPS_EACH)

    def body(*refs):
        backward_kernel(keep_up, keep_down, up_per, down_per, *refs)

    flat = pl.BlockSpec((rows, features), whole)
    return pl.pallas_call(
        body,
        out_shape=jax.ShapeDtypeStruct((rows, features), BF16),
        grid_spec=pltpu.PrefetchScalarGridSpec(
            num_scalar_prefetch=2,
            grid=(2 * STEPS_EACH,),
            in_specs=[
                flat,
                flat,
                flat,
                pl.BlockSpec(
                    (up_per, rows, size), lambda i, *_: (jnp.maximum(i - STEPS_EACH, 0), 0, 0)
                ),
                pl.BlockSpec((up_flat.shape[0] // STEPS_EACH, size), second_half),
                pl.BlockSpec((down_flat.shape[0] // STEPS_EACH, size), first_half),
            ],
            out_specs=flat,
            scratch_shapes=[
                pltpu.VMEM((hidden_blocks, rows, size), F32),
                pltpu.VMEM((width_blocks, rows, size), F32),
            ],
        ),
        compiler_params=pltpu.CompilerParams(
            dimension_semantics=("arbitrary",), vmem_limit_bytes=36 << 20
        ),
        cost_estimate=pl.CostEstimate(
            flops=4 * rows * up_flat.size, bytes_accessed=4 * up_flat.size, transcendentals=0
        ),
        name="backward",
    )(up_index.reshape(-1), down_index.reshape(-1), cot, stream, scale_plus, slope, up_flat, down_flat)


def weight_kernel(keep_down, down_index, turned_ref, cot_ref, out_ref):
    size = out_ref.shape[1]
    e = pl.program_id(0)
    right = cot_ref[...]
    for k in range(keep_down):
        h = down_index[e * keep_down + k]
        out_ref[k * size : (k + 1) * size, :] = jnp.dot(
            turned_ref[h], right, preferred_element_type=F32
        )


def weight_gradient(turned, cot, down_index):
    hidden_blocks, size, rows = turned.shape
    width_blocks, keep_down = down_index.shape

    def body(*refs):
        weight_kernel(keep_down, *refs)

    return pl.pallas_call(
        body,
        out_shape=jax.ShapeDtypeStruct((width_blocks * keep_down * size, size), F32),
        grid_spec=pltpu.PrefetchScalarGridSpec(
            num_scalar_prefetch=1,
            grid=(width_blocks,),
            in_specs=[
                pl.BlockSpec((hidden_blocks, size, rows), lambda i, *_: (0, 0, 0)),
                pl.BlockSpec((rows, size), lambda i, *_: (0, i)),
            ],
            out_specs=pl.BlockSpec((keep_down * size, size), lambda i, *_: (i, 0)),
        ),
        compiler_params=pltpu.CompilerParams(
            dimension_semantics=("arbitrary",), vmem_limit_bytes=36 << 20
        ),
        cost_estimate=pl.CostEstimate(
            flops=2 * rows * width_blocks * keep_down * size * size,
            bytes_accessed=4 * width_blocks * keep_down * size * size,
            transcendentals=0,
        ),
        name="weight_gradient",
    )(down_index.reshape(-1), turned, cot)


def lookup(step_values, table):
    rows = step_values.shape[0]
    result = jnp.broadcast_to(table[0][None, :], (rows, table.shape[1]))
    for i in range(1, table.shape[0]):
        result = jnp.where((step_values == i)[:, None], table[i][None, :], result)
    return result


def per_device(
    clean_latent,
    noise_latent,
    teacher_velocity,
    step_index,
    modulation,
    up_weight,
    up_rows,
    down_weight,
    down_rows,
):
    section_count = lax.axis_size("section")
    section_number = lax.axis_index("section")
    owner_count = lax.axis_size("dp")
    row_total, feature_count = clean_latent.shape
    size = up_weight.shape[2]
    loss_scale = 1.0 / math.sqrt(row_total * owner_count)
    up_flat = lax.all_gather(up_weight, "dp", axis=1, tiled=True)[0]
    up_index = up_rows[0]
    down_flat = down_weight[0]
    down_index = down_rows[0]
    table = modulation[0]
    fraction = (step_index.astype(F32) + 1.0) / table.shape[0]
    entry = (
        (1.0 - fraction)[:, None] * clean_latent.astype(F32)
        + fraction[:, None] * noise_latent.astype(F32)
    ).astype(BF16)
    scale_plus = 1.0 + lookup(step_index, table)
    weights = (up_flat, up_index, down_flat, down_index)

    mine = entry
    for turn in range(section_count - 1):
        (result,) = section_forward(mine, scale_plus, *weights, False)
        arrived = lax.ppermute(result, "section", [(turn, turn + 1)])
        mine = jnp.where(section_number == turn + 1, arrived, mine)
    result, slope, hidden = section_forward(mine, scale_plus, *weights, True)

    cotangent = (
        (result.astype(F32) - teacher_velocity.astype(F32)) * loss_scale
    ).astype(BF16)
    for turn in range(section_count - 1, 0, -1):
        sent = section_backward(cotangent, mine, scale_plus, slope, *weights)
        arrived = lax.ppermute(sent, "section", [(turn, turn - 1)])
        cotangent = jnp.where(section_number == turn - 1, arrived, cotangent)

    turned = jnp.swapaxes(hidden, 1, 2)
    term = weight_gradient(turned, cotangent, down_index)
    return lax.psum_scatter(term[None], "dp", scatter_dimension=1, tiled=True)


def solution(mesh):
    in_specs = (
        P("dp", None),
        P("dp", None),
        P("dp", None),
        P("dp"),
        P("section", None, None),
        P("section", "dp", None),
        P("section", None, None),
        P("section", None, None),
        P("section", None, None),
    )
    out_specs = P("section", "dp", None)
    return jax.shard_map(
        per_device, mesh=mesh, in_specs=in_specs, out_specs=out_specs, check_vma=False
    )
```

```python
import math

import jax
import jax.numpy as jnp
from jax import lax
from jax.experimental import pallas as pl
from jax.experimental.pallas import tpu as pltpu
from jax.sharding import PartitionSpec as P

EPSILON = 1e-06
F32 = jnp.float32
BF16 = jnp.bfloat16
F16 = jnp.float16
CORES = 2
CHIPS = 8
STEPS_EACH = 4
GELU_A = math.sqrt(2.0 / math.pi)
GELU_B = 0.044715


def lane_block(index, size):
    return pl.ds(pl.multiple_of(index * size, size), size)


def split_range(total, parts):
    assert total % parts == 0
    return total // parts


def gelu_parts(v):
    squared = v * v
    t = jnp.tanh(v * (GELU_A + (GELU_A * GELU_B) * squared))
    half = 0.5 * (1.0 + t)
    slope = half + (0.5 * v) * (1.0 - t * t) * (GELU_A + (3.0 * GELU_A * GELU_B) * squared)
    return v * half, slope


def forward_kernel(
    keep_up, keep_down, up_per, down_per, full, up_index, down_index, x_ref, s_ref, uw_ref, dw_ref, *rest
):
    if full:
        out_ref, slope_ref, hidden_out_ref, normed, hidden = rest
    else:
        out_ref, normed, hidden = rest
    size = normed.shape[-1]
    width_blocks = normed.shape[0]
    step = pl.program_id(0)

    @pl.when(step == 0)
    def _():
        x = x_ref[...].astype(F32)
        inverse = lax.rsqrt(jnp.mean(x * x, axis=-1, keepdims=True) + EPSILON)
        for b in range(width_blocks):
            cols = slice(b * size, (b + 1) * size)
            piece = x_ref[:, cols].astype(F32)
            normed[b] = (piece * inverse * s_ref[:, cols]).astype(BF16)

    @pl.when(step < STEPS_EACH)
    def _():
        for cc in range(up_per):
            c = step * up_per + cc
            left = jnp.concatenate(
                [normed[up_index[c * keep_up + k]] for k in range(keep_up)], axis=1
            )
            rows = keep_up * size
            pre = jnp.dot(left, uw_ref[cc * rows : (cc + 1) * rows, :], preferred_element_type=F32)
            act, slope = gelu_parts(pre)
            act = act.astype(BF16)
            hidden[c] = act
            if full:
                slope_ref[cc] = slope
                hidden_out_ref[cc] = act

    @pl.when(step >= STEPS_EACH)
    def _():
        group = 4
        for ee in range(down_per):
            e = (step - STEPS_EACH) * down_per + ee
            total = x_ref[:, lane_block(e, size)].astype(F32)
            acc = None
            for k in range(0, keep_down, group):
                left = jnp.concatenate(
                    [hidden[down_index[e * keep_down + k + q]] for q in range(group)], axis=1
                )
                first = (ee * keep_down + k) * size
                term = jnp.dot(
                    left, dw_ref[first : first + group * size, :], preferred_element_type=F32
                )
                acc = term if acc is None else acc + term
            out_ref[:, lane_block(e, size)] = (total + acc).astype(BF16)


def first_half(i, *_):
    return (jnp.minimum(i, STEPS_EACH - 1), 0)


def second_half(i, *_):
    return (jnp.maximum(i - STEPS_EACH, 0), 0)


def whole(i, *_):
    return (0, 0)


def section_forward(stream, scale_plus, up_flat, up_index, down_flat, down_index, full):
    rows, features = stream.shape
    size = up_flat.shape[1]
    hidden_blocks, keep_up = up_index.shape
    width_blocks, keep_down = down_index.shape
    up_per = split_range(hidden_blocks, STEPS_EACH)
    down_per = split_range(width_blocks, STEPS_EACH)
    out_shape = [jax.ShapeDtypeStruct((rows, features), BF16)]
    out_specs = [pl.BlockSpec((rows, features), whole)]
    if full:
        part = lambda i, *_: (jnp.minimum(i, STEPS_EACH - 1), 0, 0)
        out_shape += [
            jax.ShapeDtypeStruct((hidden_blocks, rows, size), F32),
            jax.ShapeDtypeStruct((hidden_blocks, rows, size), BF16),
        ]
        out_specs += [pl.BlockSpec((up_per, rows, size), part)] * 2

    def body(*refs):
        forward_kernel(keep_up, keep_down, up_per, down_per, full, *refs)

    return pl.pallas_call(
        body,
        out_shape=out_shape,
        grid_spec=pltpu.PrefetchScalarGridSpec(
            num_scalar_prefetch=2,
            grid=(2 * STEPS_EACH,),
            in_specs=[
                pl.BlockSpec((rows, features), whole),
                pl.BlockSpec((rows, features), whole),
                pl.BlockSpec((up_flat.shape[0] // STEPS_EACH, size), first_half),
                pl.BlockSpec((down_flat.shape[0] // STEPS_EACH, size), second_half),
            ],
            out_specs=out_specs,
            scratch_shapes=[
                pltpu.VMEM((width_blocks, rows, size), BF16),
                pltpu.VMEM((hidden_blocks, rows, size), BF16),
            ],
        ),
        compiler_params=pltpu.CompilerParams(
            dimension_semantics=("arbitrary",), vmem_limit_bytes=56 << 20
        ),
        cost_estimate=pl.CostEstimate(
            flops=4 * rows * up_flat.size, bytes_accessed=4 * up_flat.size, transcendentals=0
        ),
        name="forward_full" if full else "forward",
    )(up_index.reshape(-1), down_index.reshape(-1), stream, scale_plus, up_flat, down_flat)


def contract_last(left, right):
    return lax.dot_general(left, right, (((1,), (1,)), ((), ())), preferred_element_type=F32)


def backward_kernel(
    keep_up, keep_down, up_per, down_per, up_index, down_index,
    cot_ref, x_ref, s_ref, slope_ref, uw_ref, dw_ref, out_ref, grad_hidden, grad_normed,
):
    size = grad_hidden.shape[-1]
    width_blocks = grad_normed.shape[0]
    step = pl.program_id(0)

    @pl.when(step == 0)
    def _():
        grad_hidden[...] = jnp.zeros_like(grad_hidden)
        grad_normed[...] = jnp.zeros_like(grad_normed)

    @pl.when(step < STEPS_EACH)
    def _():
        group = 4
        for ee in range(down_per):
            e = step * down_per + ee
            left = cot_ref[:, lane_block(e, size)]
            for k in range(0, keep_down, group):
                first = (ee * keep_down + k) * size
                term = contract_last(left, dw_ref[first : first + group * size, :])
                for q in range(group):
                    h = down_index[e * keep_down + k + q]
                    grad_hidden[h] += term[:, q * size : (q + 1) * size]

    @pl.when(step >= STEPS_EACH)
    def _():
        group = 3
        for cc in range(up_per):
            c = (step - STEPS_EACH) * up_per + cc
            left = (slope_ref[cc] * grad_hidden[c]).astype(BF16)
            for k in range(0, keep_up, group):
                first = (cc * keep_up + k) * size
                term = contract_last(left, uw_ref[first : first + group * size, :])
                for q in range(group):
                    w = up_index[c * keep_up + k + q]
                    grad_normed[w] += term[:, q * size : (q + 1) * size]

    @pl.when(step == 2 * STEPS_EACH - 1)
    def _():
        x = x_ref[...].astype(F32)
        features = x.shape[1]
        inverse = lax.rsqrt(jnp.mean(x * x, axis=-1, keepdims=True) + EPSILON)
        along = jnp.zeros((x.shape[0], size), F32)
        for b in range(width_blocks):
            cols = slice(b * size, (b + 1) * size)
            scaled = grad_normed[b] * s_ref[:, cols]
            grad_normed[b] = scaled
            along += scaled * x_ref[:, cols].astype(F32)
        mean = jnp.sum(along, axis=-1, keepdims=True) * (1.0 / features)
        factor = inverse * inverse * inverse * mean
        for b in range(width_blocks):
            cols = slice(b * size, (b + 1) * size)
            grad = inverse * grad_normed[b] - x_ref[:, cols].astype(F32) * factor
            out_ref[:, cols] = (cot_ref[:, cols].astype(F32) + grad).astype(BF16)


def section_backward(cot, stream, scale_plus, slope, up_flat, up_index, down_flat, down_index):
    rows, features = stream.shape
    size = up_flat.shape[1]
    hidden_blocks, keep_up = up_index.shape
    width_blocks, keep_down = down_index.shape
    up_per = split_range(hidden_blocks, STEPS_EACH)
    down_per = split_range(width_blocks, STEPS_EACH)

    def body(*refs):
        backward_kernel(keep_up, keep_down, up_per, down_per, *refs)

    flat = pl.BlockSpec((rows, features), whole)
    return pl.pallas_call(
        body,
        out_shape=jax.ShapeDtypeStruct((rows, features), BF16),
        grid_spec=pltpu.PrefetchScalarGridSpec(
            num_scalar_prefetch=2,
            grid=(2 * STEPS_EACH,),
            in_specs=[
                flat,
                flat,
                flat,
                pl.BlockSpec(
                    (up_per, rows, size), lambda i, *_: (jnp.maximum(i - STEPS_EACH, 0), 0, 0)
                ),
                pl.BlockSpec((up_flat.shape[0] // STEPS_EACH, size), second_half),
                pl.BlockSpec((down_flat.shape[0] // STEPS_EACH, size), first_half),
            ],
            out_specs=flat,
            scratch_shapes=[
                pltpu.VMEM((hidden_blocks, rows, size), F32),
                pltpu.VMEM((width_blocks, rows, size), F32),
            ],
        ),
        compiler_params=pltpu.CompilerParams(
            dimension_semantics=("arbitrary",), vmem_limit_bytes=56 << 20
        ),
        cost_estimate=pl.CostEstimate(
            flops=4 * rows * up_flat.size, bytes_accessed=4 * up_flat.size, transcendentals=0
        ),
        name="backward",
    )(up_index.reshape(-1), down_index.reshape(-1), cot, stream, scale_plus, slope, up_flat, down_flat)


def weight_kernel(keep_down, columns, place, down_index, *refs):
    pieces, (cot_ref, keep_ref, give_ref, block_sum, largest) = refs[:-5], refs[-5:]
    size = cot_ref.shape[1] // columns
    chunk = block_sum.shape[0] // CORES
    blocks = block_sum.shape[0] // size
    far = pl.program_id(0)
    y, z, core = place[0], place[1], place[2]
    chips = pl.num_programs(0)
    owner = y * chips + lax.rem(z + far, chips)

    @pl.when(far == 0)
    def _():
        largest[...] = jnp.zeros_like(largest)

    top = largest[...]
    for g in range(blocks):
        b = owner * blocks + g
        e = lax.div(b, keep_down) - y * columns
        h = down_index[b]
        left = jnp.concatenate([piece[h] for piece in pieces], axis=1)
        term = jnp.dot(left, cot_ref[:, lane_block(e, size)], preferred_element_type=F32)
        block_sum[g * size : (g + 1) * size, :] = term
        top = jnp.maximum(top, jnp.max(jnp.abs(term).reshape(-1, 8, size), axis=0))
    largest[...] = top
    rows = pl.ds(pl.multiple_of(far * chunk, 8), chunk)
    keep_ref[rows, :] = block_sum[pl.ds(pl.multiple_of(core * chunk, 8), chunk), :]
    give_ref[rows, :] = block_sum[pl.ds(pl.multiple_of((1 - core) * chunk, 8), chunk), :]

    @pl.when(far == chips - 1)
    def _():
        peak = jnp.broadcast_to(jnp.max(top), (8, size))
        keep_ref[chips * chunk :, :] = peak
        give_ref[chips * chunk :, :] = peak


def weight_gradient(pieces, cot, down_index, place, chips, owners):
    hidden_blocks, size, rows = pieces[0].shape
    width_blocks, keep_down = down_index.shape
    columns = cot.shape[1] // size
    total_rows = width_blocks * keep_down * size
    chunk = split_range(total_rows, owners)

    def body(*refs):
        weight_kernel(keep_down, columns, *refs)

    held = pl.BlockSpec(
        (hidden_blocks, size, rows), lambda i, *_: (0, 0, 0), pipeline_mode=pl.Buffered(1)
    )
    shape = jax.ShapeDtypeStruct((chips * chunk + 8, size), F32)
    return pl.pallas_call(
        body,
        out_shape=[shape, shape],
        grid_spec=pltpu.PrefetchScalarGridSpec(
            num_scalar_prefetch=2,
            grid=(chips,),
            in_specs=[held] * len(pieces) + [pl.BlockSpec(cot.shape, whole)],
            out_specs=[pl.BlockSpec(shape.shape, whole)] * 2,
            scratch_shapes=[
                pltpu.VMEM((CORES * chunk, size), F32),
                pltpu.VMEM((8, size), F32),
            ],
        ),
        compiler_params=pltpu.CompilerParams(
            dimension_semantics=("arbitrary",), vmem_limit_bytes=40 << 20
        ),
        cost_estimate=pl.CostEstimate(
            flops=2 * rows * len(pieces) * chips * CORES * chunk * size,
            bytes_accessed=2 * len(pieces) * pieces[0].size,
            transcendentals=0,
        ),
        name="weight_gradient",
    )(place, down_index.reshape(-1), *pieces, cot)


def dp_route(rows, chips, move):
    owners = rows * chips * CORES
    route = []
    for source in range(owners):
        y, rest = divmod(source, chips * CORES)
        z, core = divmod(rest, CORES)
        y, z, core = move(y, z, core)
        route.append((source, (y % rows * chips + z % chips) * CORES + core % CORES))
    return route


def hidden_pieces(turned, rows, chips):
    pieces = [turned]
    for r in range(1, rows):
        route = dp_route(rows, chips, lambda y, z, core: (y - r, z, core))
        pieces.append(lax.ppermute(turned, "dp", route))
    return pieces


def reduce_weight_gradient(pieces, cot, down_index, rows, chips):
    owners = rows * chips * CORES
    number = lax.axis_index("dp")
    y = lax.div(number, chips * CORES)
    place = jnp.stack([y, lax.rem(lax.div(number, CORES), chips), lax.rem(number, CORES)])
    columns = split_range(cot.shape[1], rows)
    received = []
    for r in range(rows):
        first = lax.rem(y + rows - r, rows) * columns
        part = lax.dynamic_slice_in_dim(cot, first, columns, 1)
        if r:
            route = dp_route(rows, chips, lambda y, z, core: (y - r, z, core))
            part = lax.ppermute(part, "dp", route)
        received.append(part)
    keep, give = weight_gradient(
        pieces, jnp.concatenate(received, axis=0), down_index, place, chips, owners
    )
    swap = dp_route(rows, chips, lambda y, z, core: (y, z, core + 1))
    total = keep + lax.ppermute(give, "dp", swap)
    chunk = split_range(keep.shape[0] - 8, chips)
    bound = jnp.maximum(total[chips * chunk : chips * chunk + 1], 1e-30)
    power = jnp.floor(13.0 - jnp.log2(bound))
    factor = jnp.exp2(power)
    tag = jnp.broadcast_to(power, (16, power.shape[1])).astype(F16)
    result = total[:chunk]
    for r in range(1, chips):
        coded = (total[r * chunk : (r + 1) * chunk] * factor).astype(F16)
        route = dp_route(rows, chips, lambda y, z, core: (y, z + r, core))
        got = lax.ppermute(jnp.concatenate([coded, tag], axis=0), "dp", route)
        got = got.astype(F32)
        result = result + got[:chunk] * jnp.exp2(-got[chunk : chunk + 1])
    return result


def lookup(step_values, table):
    rows = step_values.shape[0]
    result = jnp.broadcast_to(table[0][None, :], (rows, table.shape[1]))
    for i in range(1, table.shape[0]):
        result = jnp.where((step_values == i)[:, None], table[i][None, :], result)
    return result


def per_device(
    clean_latent,
    noise_latent,
    teacher_velocity,
    step_index,
    modulation,
    up_weight,
    up_rows,
    down_weight,
    down_rows,
):
    section_count = lax.axis_size("section")
    section_number = lax.axis_index("section")
    owner_count = lax.axis_size("dp")
    row_total, feature_count = clean_latent.shape
    size = up_weight.shape[2]
    loss_scale = 1.0 / math.sqrt(row_total * owner_count)
    up_flat = lax.all_gather(up_weight, "dp", axis=1, tiled=True)[0]
    up_index = up_rows[0]
    down_flat = down_weight[0]
    down_index = down_rows[0]
    table = modulation[0]
    fraction = (step_index.astype(F32) + 1.0) / table.shape[0]
    entry = (
        (1.0 - fraction)[:, None] * clean_latent.astype(F32)
        + fraction[:, None] * noise_latent.astype(F32)
    ).astype(BF16)
    scale_plus = 1.0 + lookup(step_index, table)
    weights = (up_flat, up_index, down_flat, down_index)

    mine = entry
    for turn in range(section_count - 1):
        (result,) = section_forward(mine, scale_plus, *weights, False)
        arrived = lax.ppermute(result, "section", [(turn, turn + 1)])
        mine = jnp.where(section_number == turn + 1, arrived, mine)
    result, slope, hidden = section_forward(mine, scale_plus, *weights, True)

    cotangent = (
        (result.astype(F32) - teacher_velocity.astype(F32)) * loss_scale
    ).astype(BF16)
    rows = split_range(owner_count, CHIPS * CORES)
    pieces = None
    for turn in range(section_count - 1, 0, -1):
        sent = section_backward(cotangent, mine, scale_plus, slope, *weights)
        if pieces is None:
            hidden, sent = lax.optimization_barrier((hidden, sent))
            pieces = hidden_pieces(jnp.swapaxes(hidden, 1, 2), rows, CHIPS)
        arrived = lax.ppermute(sent, "section", [(turn, turn - 1)])
        cotangent = jnp.where(section_number == turn - 1, arrived, cotangent)

    return reduce_weight_gradient(pieces, cotangent, down_index, rows, CHIPS)[None]


def solution(mesh):
    in_specs = (
        P("dp", None),
        P("dp", None),
        P("dp", None),
        P("dp"),
        P("section", None, None),
        P("section", "dp", None),
        P("section", None, None),
        P("section", None, None),
        P("section", None, None),
    )
    out_specs = P("section", "dp", None)
    return jax.shard_map(
        per_device, mesh=mesh, in_specs=in_specs, out_specs=out_specs, check_vma=False
    )
```

```python
import math

import jax
import jax.numpy as jnp
from jax import lax
from jax.experimental import pallas as pl
from jax.experimental.pallas import tpu as pltpu
from jax.sharding import PartitionSpec as P

EPSILON = 1e-06
F32 = jnp.float32
BF16 = jnp.bfloat16
F16 = jnp.float16
CORES = 2
CHIPS = 8
UP_UNROLL = 4
DOWN_UNROLL = 3
LIMIT = 12 << 20
PARTS = 4
ROWS = 4
GELU_A = math.sqrt(2.0 / math.pi)
GELU_B = 0.044715


def lane_block(index, size):
    return pl.ds(pl.multiple_of(index * size, size), size)


def split_range(total, parts):
    assert total % parts == 0
    return total // parts


def gelu_parts(v):
    squared = v * v
    t = jnp.tanh(v * (GELU_A + (GELU_A * GELU_B) * squared))
    half = 0.5 * (1.0 + t)
    slope = half + (0.5 * v) * (1.0 - t * t) * (GELU_A + (3.0 * GELU_A * GELU_B) * squared)
    return v * half, slope


def pick(take, arrived_ref, held_ref, out_ref):
    @pl.when(take)
    def _():
        out_ref[...] = arrived_ref[...]

    @pl.when(jnp.logical_not(take))
    def _():
        out_ref[...] = held_ref[...]


def forward_kernel(keep_up, keep_down, turn, last, loss_scale, *refs):
    refs = list(refs)
    up_index, down_index = refs[:2]
    del refs[:2]
    if turn:
        section, arrived_ref, held_ref = refs[:3]
        del refs[:3]
    else:
        x_ref = refs.pop(0)
    s_ref, uw_ref, dw_ref = refs[:3]
    del refs[:3]
    if last:
        teacher_ref = refs.pop(0)
    out_ref = refs.pop(0)
    if turn:
        x_ref = refs.pop(0)
        pick(section[0] == turn, arrived_ref, held_ref, x_ref)
    copies = []
    if last:
        slope_ref, hidden, normed = refs
    elif turn:
        normed, hidden = refs
    else:
        uw_to, dw_to, normed, hidden, arrival = refs
        for source, target in ((uw_ref, uw_to), (dw_ref, dw_to)):
            rows = source.shape[0] // PARTS
            for p in range(PARTS):
                span = pl.ds(p * rows, rows)
                copy = pltpu.make_async_copy(
                    source.at[span, :], target.at[span, :], arrival.at[len(copies)]
                )
                copy.start()
                copies.append(copy)
        uw_ref, dw_ref = uw_to, dw_to
    size = normed.shape[-1]
    width_blocks = normed.shape[0]
    hidden_blocks = hidden.shape[0]
    x = x_ref[...].astype(F32)
    inverse = lax.rsqrt(jnp.mean(x * x, axis=-1, keepdims=True) + EPSILON)
    for b in range(width_blocks):
        cols = slice(b * size, (b + 1) * size)
        piece = x_ref[:, cols].astype(F32)
        normed[b] = (piece * inverse * s_ref[:, cols]).astype(BF16)

    rows = keep_up * size

    def up_step(step, carry):
        for cc in range(UP_UNROLL):
            c = step * UP_UNROLL + cc
            left = jnp.concatenate(
                [normed[up_index[c * keep_up + k]] for k in range(keep_up)], axis=1
            )
            first = pl.multiple_of(c * rows, rows)
            pre = jnp.dot(left, uw_ref[pl.ds(first, rows), :], preferred_element_type=F32)
            act, slope = gelu_parts(pre)
            hidden[c] = act.astype(BF16)
            if last:
                slope_ref[c] = slope
        return carry

    group = 4

    def down_step(step, carry):
        for ee in range(DOWN_UNROLL):
            e = step * DOWN_UNROLL + ee
            acc = x_ref[:, lane_block(e, size)].astype(F32)
            for k in range(0, keep_down, group):
                left = jnp.concatenate(
                    [hidden[down_index[e * keep_down + k + q]] for q in range(group)], axis=1
                )
                first = pl.multiple_of((e * keep_down + k) * size, group * size)
                acc = acc + jnp.dot(
                    left, dw_ref[pl.ds(first, group * size), :], preferred_element_type=F32
                )
            result = acc.astype(BF16)
            if last:
                target = teacher_ref[:, lane_block(e, size)].astype(F32)
                result = ((result.astype(F32) - target) * loss_scale).astype(BF16)
            out_ref[:, lane_block(e, size)] = result
        return carry

    for step_of, count, waits in (
        (up_step, hidden_blocks // UP_UNROLL, copies[:PARTS]),
        (down_step, width_blocks // DOWN_UNROLL, copies[PARTS:]),
    ):
        if waits:
            per = split_range(count, PARTS)
            for p, copy in enumerate(waits):
                copy.wait()
                lax.fori_loop(p * per, (p + 1) * per, step_of, 0)
        else:
            lax.fori_loop(0, count, step_of, 0)


def whole(i, *_):
    return (0, 0)


SMEM = pl.BlockSpec(memory_space=pltpu.SMEM)
VMEM = pl.BlockSpec(memory_space=pltpu.VMEM)


def section_forward(turn, last, loss_scale, states, scale_plus, weights, indices, teacher):
    rows, features = scale_plus.shape
    size = weights[0].shape[1]
    hidden_blocks, keep_up = indices[0].shape
    width_blocks, keep_down = indices[1].shape
    stream = jax.ShapeDtypeStruct((rows, features), BF16)
    out_shape = [stream]
    scratch = [pltpu.VMEM((width_blocks, rows, size), BF16)]
    hidden = (hidden_blocks, rows, size)
    operands = [index.reshape(-1) for index in indices] + list(states)
    operands += [scale_plus, *weights]
    in_specs = [SMEM, SMEM] + ([SMEM, VMEM, VMEM] if turn else [VMEM]) + [VMEM]
    in_specs += [VMEM, VMEM] if turn else [pl.BlockSpec(memory_space=pltpu.HBM)] * 2
    if last:
        operands.append(teacher)
        in_specs.append(VMEM)
    if turn:
        out_shape.append(stream)
    if last:
        out_shape += [jax.ShapeDtypeStruct(hidden, F32), jax.ShapeDtypeStruct(hidden, BF16)]
    else:
        scratch.append(pltpu.VMEM(hidden, BF16))
    if not turn:
        out_shape += [jax.ShapeDtypeStruct(w.shape, w.dtype) for w in weights]
        scratch.append(pltpu.SemaphoreType.DMA((2 * PARTS,)))

    def body(*refs):
        forward_kernel(keep_up, keep_down, turn, last, loss_scale, *refs)

    return pl.pallas_call(
        body,
        out_shape=out_shape,
        in_specs=in_specs,
        out_specs=[VMEM] * len(out_shape),
        scratch_shapes=scratch,
        compiler_params=pltpu.CompilerParams(vmem_limit_bytes=LIMIT if turn else 40 << 20),
        cost_estimate=pl.CostEstimate(
            flops=4 * rows * weights[0].size, bytes_accessed=4 * features, transcendentals=0
        ),
        name=f"forward_{turn}",
    )(*operands)


def contract_last(left, right):
    return lax.dot_general(left, right, (((1,), (1,)), ((), ())), preferred_element_type=F32)


def backward_kernel(
    keep_up, keep_down, turn, first_turn, up_index, down_index, *refs
):
    if first_turn:
        cot_ref, x_ref, s_ref, slope_ref, uw_ref, dw_ref, out_ref, grad_hidden, grad_normed = refs
    else:
        section, arrived_ref, held_ref, *refs = refs
        x_ref, s_ref, slope_ref, uw_ref, dw_ref, out_ref, cot_ref, grad_hidden, grad_normed = refs
        pick(section[0] == turn, arrived_ref, held_ref, cot_ref)
    size = grad_hidden.shape[-1]
    width_blocks = grad_normed.shape[0]
    hidden_blocks = grad_hidden.shape[0]
    grad_hidden[...] = jnp.zeros_like(grad_hidden)
    grad_normed[...] = jnp.zeros_like(grad_normed)
    group = 4

    def down_step(step, carry):
        for ee in range(DOWN_UNROLL):
            e = step * DOWN_UNROLL + ee
            left = cot_ref[:, lane_block(e, size)]
            for k in range(0, keep_down, group):
                first = pl.multiple_of((e * keep_down + k) * size, group * size)
                term = contract_last(left, dw_ref[pl.ds(first, group * size), :])
                for q in range(group):
                    h = down_index[e * keep_down + k + q]
                    grad_hidden[h] += term[:, q * size : (q + 1) * size]
        return carry

    lax.fori_loop(0, width_blocks // DOWN_UNROLL, down_step, 0)
    part = 3

    def up_step(step, carry):
        for cc in range(UP_UNROLL):
            c = step * UP_UNROLL + cc
            left = (slope_ref[c] * grad_hidden[c]).astype(BF16)
            for k in range(0, keep_up, part):
                first = pl.multiple_of((c * keep_up + k) * size, part * size)
                term = contract_last(left, uw_ref[pl.ds(first, part * size), :])
                for q in range(part):
                    w = up_index[c * keep_up + k + q]
                    grad_normed[w] += term[:, q * size : (q + 1) * size]
        return carry

    lax.fori_loop(0, hidden_blocks // UP_UNROLL, up_step, 0)
    x = x_ref[...].astype(F32)
    features = x.shape[1]
    inverse = lax.rsqrt(jnp.mean(x * x, axis=-1, keepdims=True) + EPSILON)
    along = jnp.zeros((x.shape[0], size), F32)
    for b in range(width_blocks):
        cols = slice(b * size, (b + 1) * size)
        scaled = grad_normed[b] * s_ref[:, cols]
        grad_normed[b] = scaled
        along += scaled * x_ref[:, cols].astype(F32)
    mean = jnp.sum(along, axis=-1, keepdims=True) * (1.0 / features)
    factor = inverse * inverse * inverse * mean
    for b in range(width_blocks):
        cols = slice(b * size, (b + 1) * size)
        grad = inverse * grad_normed[b] - x_ref[:, cols].astype(F32) * factor
        out_ref[:, cols] = (cot_ref[:, cols].astype(F32) + grad).astype(BF16)


def section_backward(turn, first_turn, states, stream, scale_plus, slope, weights, indices):
    rows, features = stream.shape
    size = weights[0].shape[1]
    hidden_blocks, keep_up = indices[0].shape
    width_blocks, keep_down = indices[1].shape

    def body(*refs):
        backward_kernel(keep_up, keep_down, turn, first_turn, *refs)

    result = jax.ShapeDtypeStruct((rows, features), BF16)
    out_shape = [result] if first_turn else [result, result]
    in_specs = [SMEM, SMEM] + ([VMEM] if first_turn else [SMEM, VMEM, VMEM]) + [VMEM] * 5
    return pl.pallas_call(
        body,
        out_shape=out_shape,
        in_specs=in_specs,
        out_specs=[VMEM] * len(out_shape),
        scratch_shapes=[
            pltpu.VMEM((hidden_blocks, rows, size), F32),
            pltpu.VMEM((width_blocks, rows, size), F32),
        ],
        compiler_params=pltpu.CompilerParams(vmem_limit_bytes=LIMIT),
        cost_estimate=pl.CostEstimate(flops=1000000, bytes_accessed=100000, transcendentals=0),
        name=f"backward_{turn}",
    )(*[index.reshape(-1) for index in indices], *states, stream, scale_plus, slope, *weights)


def turn_kernel(source_ref, out_ref):
    def step(h, carry):
        for i in range(4):
            out_ref[h * 4 + i] = source_ref[h * 4 + i].T
        return carry

    lax.fori_loop(0, source_ref.shape[0] // 4, step, 0)


def turn_hidden(hidden):
    blocks, rows, size = hidden.shape
    return pl.pallas_call(
        turn_kernel,
        out_shape=jax.ShapeDtypeStruct((blocks, size, rows), hidden.dtype),
        in_specs=[VMEM],
        out_specs=VMEM,
        compiler_params=pltpu.CompilerParams(vmem_limit_bytes=LIMIT),
        cost_estimate=pl.CostEstimate(
            flops=20000 * hidden.size, bytes_accessed=4 * hidden.size, transcendentals=0
        ),
        name="turn_hidden",
    )(hidden)


def weight_kernel(keep_down, columns, place, down_index, *refs):
    pieces, (cot_ref, keep_ref, give_ref, block_sum, largest) = refs[:-5], refs[-5:]
    size = cot_ref.shape[1] // columns
    chunk = block_sum.shape[0] // CORES
    blocks = block_sum.shape[0] // size
    far = pl.program_id(0)
    y, z, core = place[0], place[1], place[2]
    chips = pl.num_programs(0)
    owner = y * chips + lax.rem(z + far, chips)

    @pl.when(far == 0)
    def _():
        largest[...] = jnp.zeros_like(largest)

    top = largest[...]
    for g in range(blocks):
        b = owner * blocks + g
        e = lax.div(b, keep_down) - y * columns
        h = down_index[b]
        near, low, high = pieces[:-2], pieces[-2], pieces[-1]
        half = low.shape[0]
        far_piece = jnp.where(
            h < half, low[jnp.minimum(h, half - 1)], high[jnp.maximum(h - half, 0)]
        )
        left = jnp.concatenate([piece[h] for piece in near] + [far_piece], axis=1)
        term = jnp.dot(left, cot_ref[:, lane_block(e, size)], preferred_element_type=F32)
        block_sum[g * size : (g + 1) * size, :] = term
        top = jnp.maximum(top, jnp.max(jnp.abs(term).reshape(-1, 8, size), axis=0))
    largest[...] = top
    rows = pl.ds(pl.multiple_of(far * chunk, 8), chunk)
    keep_ref[rows, :] = block_sum[pl.ds(pl.multiple_of(core * chunk, 8), chunk), :]
    give_ref[rows, :] = block_sum[pl.ds(pl.multiple_of((1 - core) * chunk, 8), chunk), :]

    @pl.when(far == chips - 1)
    def _():
        peak = jnp.broadcast_to(jnp.max(top), (8, size))
        keep_ref[chips * chunk :, :] = peak
        give_ref[chips * chunk :, :] = peak


def weight_gradient(pieces, cot, down_index, place, chips, owners):
    size = pieces[0].shape[1]
    width_blocks, keep_down = down_index.shape
    columns = cot.shape[1] // size
    total_rows = width_blocks * keep_down * size
    chunk = split_range(total_rows, owners)

    def body(*refs):
        weight_kernel(keep_down, columns, *refs)

    held = [
        pl.BlockSpec(piece.shape, lambda i, *_: (0, 0, 0), pipeline_mode=pl.Buffered(1))
        for piece in pieces
    ]
    shape = jax.ShapeDtypeStruct((chips * chunk + 8, size), F32)
    return pl.pallas_call(
        body,
        out_shape=[shape, shape],
        grid_spec=pltpu.PrefetchScalarGridSpec(
            num_scalar_prefetch=2,
            grid=(chips,),
            in_specs=held + [pl.BlockSpec(cot.shape, whole)],
            out_specs=[pl.BlockSpec(shape.shape, whole)] * 2,
            scratch_shapes=[
                pltpu.VMEM((CORES * chunk, size), F32),
                pltpu.VMEM((8, size), F32),
            ],
        ),
        compiler_params=pltpu.CompilerParams(
            dimension_semantics=("arbitrary",), vmem_limit_bytes=40 << 20
        ),
        cost_estimate=pl.CostEstimate(
            flops=2 * cot.shape[0] * chips * CORES * chunk * size,
            bytes_accessed=2 * len(pieces) * pieces[0].size,
            transcendentals=0,
        ),
        name="weight_gradient",
    )(place, down_index.reshape(-1), *pieces, cot)


def dp_route(rows, chips, move):
    owners = rows * chips * CORES
    route = []
    for source in range(owners):
        y, rest = divmod(source, chips * CORES)
        z, core = divmod(rest, CORES)
        y, z, core = move(y, z, core)
        route.append((source, (y % rows * chips + z % chips) * CORES + core % CORES))
    return route


def hidden_pieces(turned, rows, chips):
    assert rows == ROWS
    half = turned.shape[0] // 2
    down = dp_route(rows, chips, lambda y, z, core: (y - 1, z, core))
    up = dp_route(rows, chips, lambda y, z, core: (y + 1, z, core))
    after = lax.ppermute(turned, "dp", down)
    before = lax.ppermute(turned, "dp", up)
    low = lax.ppermute(after[:half], "dp", down)
    high = lax.ppermute(before[half:], "dp", up)
    return [turned, after, before, low, high]


def reduce_weight_gradient(pieces, cot, down_index, rows, chips):
    owners = rows * chips * CORES
    number = lax.axis_index("dp")
    y = lax.div(number, chips * CORES)
    place = jnp.stack([y, lax.rem(lax.div(number, CORES), chips), lax.rem(number, CORES)])
    columns = split_range(cot.shape[1], rows)
    received = []
    for r in (0, 1, rows - 1, 2):
        first = lax.rem(y + rows - r, rows) * columns
        part = lax.dynamic_slice_in_dim(cot, first, columns, 1)
        if r:
            route = dp_route(rows, chips, lambda y, z, core: (y - r, z, core))
            part = lax.ppermute(part, "dp", route)
        received.append(part)
    keep, give = weight_gradient(
        pieces, jnp.concatenate(received, axis=0), down_index, place, chips, owners
    )
    swap = dp_route(rows, chips, lambda y, z, core: (y, z, core + 1))
    total = keep + lax.ppermute(give, "dp", swap)
    chunk = split_range(keep.shape[0] - 8, chips)
    bound = jnp.maximum(total[chips * chunk : chips * chunk + 1], 1e-30)
    power = jnp.floor(13.0 - jnp.log2(bound))
    factor = jnp.exp2(power)
    tag = jnp.broadcast_to(power, (16, power.shape[1])).astype(F16)
    result = total[:chunk]
    for r in range(1, chips):
        coded = (total[r * chunk : (r + 1) * chunk] * factor).astype(F16)
        route = dp_route(rows, chips, lambda y, z, core: (y, z + r, core))
        got = lax.ppermute(jnp.concatenate([coded, tag], axis=0), "dp", route)
        got = got.astype(F32)
        result = result + got[:chunk] * jnp.exp2(-got[chunk : chunk + 1])
    return result


def lookup(step_values, table):
    rows = step_values.shape[0]
    result = jnp.broadcast_to(table[0][None, :], (rows, table.shape[1]))
    for i in range(1, table.shape[0]):
        result = jnp.where((step_values == i)[:, None], table[i][None, :], result)
    return result


def per_device(
    clean_latent,
    noise_latent,
    teacher_velocity,
    step_index,
    modulation,
    up_weight,
    up_rows,
    down_weight,
    down_rows,
):
    section_count = lax.axis_size("section")
    section_number = lax.axis_index("section")
    owner_count = lax.axis_size("dp")
    row_total, feature_count = clean_latent.shape
    size = up_weight.shape[2]
    loss_scale = 1.0 / math.sqrt(row_total * owner_count)
    up_flat = lax.all_gather(up_weight, "dp", axis=1, tiled=True)[0]
    up_index = up_rows[0]
    down_flat = down_weight[0]
    down_index = down_rows[0]
    table = modulation[0]
    fraction = (step_index.astype(F32) + 1.0) / table.shape[0]
    entry = (
        (1.0 - fraction)[:, None] * clean_latent.astype(F32)
        + fraction[:, None] * noise_latent.astype(F32)
    ).astype(BF16)
    scale_plus = 1.0 + lookup(step_index, table)
    indices = (up_index, down_index)
    section = section_number.reshape(1).astype(jnp.int32)
    section, entry = lax.optimization_barrier((section, entry))

    result, *weights = section_forward(
        0, False, loss_scale, (entry,), scale_plus, (up_flat, down_flat), indices, None
    )
    mine = entry
    for turn in range(1, section_count):
        last = turn == section_count - 1
        arrived = lax.ppermute(result, "section", [(turn - 1, turn)])
        result, mine, *kept = section_forward(
            turn, last, loss_scale, (section, arrived, mine), scale_plus, weights, indices,
            teacher_velocity,
        )
    slope, hidden = kept
    cotangent = result
    rows = split_range(owner_count, CHIPS * CORES)
    states = (cotangent,)
    for turn in range(section_count - 1, 0, -1):
        first_turn = turn == section_count - 1
        sent, *moved = section_backward(
            turn, first_turn, states, mine, scale_plus, slope, weights, indices
        )
        if first_turn:
            hidden, sent = lax.optimization_barrier((hidden, sent))
            pieces = hidden_pieces(turn_hidden(hidden), rows, CHIPS)
        else:
            (cotangent,) = moved
        arrived = lax.ppermute(sent, "section", [(turn, turn - 1)])
        states = (section, arrived, cotangent)
    cotangent = jnp.where(section_number == 0, arrived, cotangent)

    return reduce_weight_gradient(pieces, cotangent, down_index, rows, CHIPS)[None]


def solution(mesh):
    in_specs = (
        P("dp", None),
        P("dp", None),
        P("dp", None),
        P("dp"),
        P("section", None, None),
        P("section", "dp", None),
        P("section", None, None),
        P("section", None, None),
        P("section", None, None),
    )
    out_specs = P("section", "dp", None)
    return jax.shard_map(
        per_device, mesh=mesh, in_specs=in_specs, out_specs=out_specs, check_vma=False
    )
```

```python
import math

import jax
import jax.numpy as jnp
from jax import lax
from jax.experimental import pallas as pl
from jax.experimental.pallas import tpu as pltpu
from jax.sharding import PartitionSpec as P

EPSILON = 1e-06
F32 = jnp.float32
BF16 = jnp.bfloat16
F16 = jnp.float16
CORES = 2
CHIPS = 8
UP_UNROLL = 4
DOWN_UNROLL = 3
LIMIT = 12 << 20
PARTS = 4
ROWS = 4
GELU_A = math.sqrt(2.0 / math.pi)
GELU_B = 0.044715


def lane_block(index, size):
    return pl.ds(pl.multiple_of(index * size, size), size)


def split_range(total, parts):
    assert total % parts == 0
    return total // parts


def gelu_parts(v):
    squared = v * v
    t = jnp.tanh(v * (GELU_A + (GELU_A * GELU_B) * squared))
    half = 0.5 * (1.0 + t)
    slope = half + (0.5 * v) * (1.0 - t * t) * (GELU_A + (3.0 * GELU_A * GELU_B) * squared)
    return v * half, slope


def pick(take, arrived_ref, held_ref, out_ref):
    @pl.when(take)
    def _():
        out_ref[...] = arrived_ref[...]

    @pl.when(jnp.logical_not(take))
    def _():
        out_ref[...] = held_ref[...]


def forward_kernel(keep_up, keep_down, turn, last, loss_scale, *refs):
    refs = list(refs)
    up_index, down_index = refs[:2]
    del refs[:2]
    if turn:
        section, arrived_ref, held_ref = refs[:3]
        del refs[:3]
    else:
        x_ref = refs.pop(0)
    s_ref, uw_ref, dw_ref = refs[:3]
    del refs[:3]
    if last:
        teacher_ref = refs.pop(0)
    out_ref = refs.pop(0)
    if turn:
        x_ref = refs.pop(0)
        pick(section[0] == turn, arrived_ref, held_ref, x_ref)
    copies = []
    if last:
        slope_ref, turned_ref, normed, hidden = refs
    elif turn:
        normed, hidden = refs
    else:
        uw_to, dw_to, normed, hidden, arrival = refs
        for source, target in ((uw_ref, uw_to), (dw_ref, dw_to)):
            rows = source.shape[0] // PARTS
            for p in range(PARTS):
                span = pl.ds(p * rows, rows)
                copy = pltpu.make_async_copy(
                    source.at[span, :], target.at[span, :], arrival.at[len(copies)]
                )
                copies.append(copy)
        for copy in copies[:PARTS]:
            copy.start()
        uw_ref, dw_ref = uw_to, dw_to
    size = normed.shape[-1]
    width_blocks = normed.shape[0]
    hidden_blocks = hidden.shape[0]
    x = x_ref[...].astype(F32)
    inverse = lax.rsqrt(jnp.mean(x * x, axis=-1, keepdims=True) + EPSILON)
    for b in range(width_blocks):
        cols = slice(b * size, (b + 1) * size)
        piece = x_ref[:, cols].astype(F32)
        normed[b] = (piece * inverse * s_ref[:, cols]).astype(BF16)

    rows = keep_up * size

    def up_step(step, carry):
        for cc in range(UP_UNROLL):
            c = step * UP_UNROLL + cc
            left = jnp.concatenate(
                [normed[up_index[c * keep_up + k]] for k in range(keep_up)], axis=1
            )
            first = pl.multiple_of(c * rows, rows)
            pre = jnp.dot(left, uw_ref[pl.ds(first, rows), :], preferred_element_type=F32)
            act, slope = gelu_parts(pre)
            act = act.astype(BF16)
            hidden[c] = act
            if last:
                slope_ref[c] = slope
                turned_ref[c] = act.T
        return carry

    group = 4

    def down_step(step, carry):
        for ee in range(DOWN_UNROLL):
            e = step * DOWN_UNROLL + ee
            acc = x_ref[:, lane_block(e, size)].astype(F32)
            for k in range(0, keep_down, group):
                left = jnp.concatenate(
                    [hidden[down_index[e * keep_down + k + q]] for q in range(group)], axis=1
                )
                first = pl.multiple_of((e * keep_down + k) * size, group * size)
                acc = acc + jnp.dot(
                    left, dw_ref[pl.ds(first, group * size), :], preferred_element_type=F32
                )
            result = acc.astype(BF16)
            if last:
                target = teacher_ref[:, lane_block(e, size)].astype(F32)
                result = ((result.astype(F32) - target) * loss_scale).astype(BF16)
            out_ref[:, lane_block(e, size)] = result
        return carry

    for step_of, count, waits in (
        (up_step, hidden_blocks // UP_UNROLL, copies[:PARTS]),
        (down_step, width_blocks // DOWN_UNROLL, copies[PARTS:]),
    ):
        if waits:
            per = split_range(count, PARTS)
            for p, copy in enumerate(waits):
                copy.wait()
                if step_of is up_step:
                    copies[PARTS + p].start()
                lax.fori_loop(p * per, (p + 1) * per, step_of, 0)
        else:
            lax.fori_loop(0, count, step_of, 0)


def whole(i, *_):
    return (0, 0)


SMEM = pl.BlockSpec(memory_space=pltpu.SMEM)
VMEM = pl.BlockSpec(memory_space=pltpu.VMEM)


def section_forward(turn, last, loss_scale, states, scale_plus, weights, indices, teacher):
    rows, features = scale_plus.shape
    size = weights[0].shape[1]
    hidden_blocks, keep_up = indices[0].shape
    width_blocks, keep_down = indices[1].shape
    stream = jax.ShapeDtypeStruct((rows, features), BF16)
    out_shape = [stream]
    scratch = [pltpu.VMEM((width_blocks, rows, size), BF16)]
    hidden = (hidden_blocks, rows, size)
    operands = [index.reshape(-1) for index in indices] + list(states)
    operands += [scale_plus, *weights]
    in_specs = [SMEM, SMEM] + ([SMEM, VMEM, VMEM] if turn else [VMEM]) + [VMEM]
    in_specs += [VMEM, VMEM] if turn else [pl.BlockSpec(memory_space=pltpu.HBM)] * 2
    if last:
        operands.append(teacher)
        in_specs.append(VMEM)
    if turn:
        out_shape.append(stream)
    if last:
        turned = (hidden_blocks, size, rows)
        out_shape += [jax.ShapeDtypeStruct(hidden, F32), jax.ShapeDtypeStruct(turned, BF16)]
    scratch.append(pltpu.VMEM(hidden, BF16))
    if not turn:
        out_shape += [jax.ShapeDtypeStruct(w.shape, w.dtype) for w in weights]
        scratch.append(pltpu.SemaphoreType.DMA((2 * PARTS,)))

    def body(*refs):
        forward_kernel(keep_up, keep_down, turn, last, loss_scale, *refs)

    return pl.pallas_call(
        body,
        out_shape=out_shape,
        in_specs=in_specs,
        out_specs=[VMEM] * len(out_shape),
        scratch_shapes=scratch,
        compiler_params=pltpu.CompilerParams(vmem_limit_bytes=LIMIT if turn else 31 << 20),
        cost_estimate=pl.CostEstimate(
            flops=4 * rows * weights[0].size, bytes_accessed=4 * features, transcendentals=0
        ),
        name=f"forward_{turn}",
    )(*operands)


def contract_last(left, right):
    return lax.dot_general(left, right, (((1,), (1,)), ((), ())), preferred_element_type=F32)


def backward_kernel(
    keep_up, keep_down, turn, first_turn, up_index, down_index, *refs
):
    if first_turn:
        cot_ref, x_ref, s_ref, slope_ref, uw_ref, dw_ref, out_ref, grad_hidden, grad_normed = refs
    else:
        section, arrived_ref, held_ref, *refs = refs
        x_ref, s_ref, slope_ref, uw_ref, dw_ref, out_ref, cot_ref, grad_hidden, grad_normed = refs
        pick(section[0] == turn, arrived_ref, held_ref, cot_ref)
    size = grad_hidden.shape[-1]
    width_blocks = grad_normed.shape[0]
    hidden_blocks = grad_hidden.shape[0]
    grad_hidden[...] = jnp.zeros_like(grad_hidden)
    grad_normed[...] = jnp.zeros_like(grad_normed)
    group = 4

    def down_step(step, carry):
        for ee in range(DOWN_UNROLL):
            e = step * DOWN_UNROLL + ee
            left = cot_ref[:, lane_block(e, size)]
            for k in range(0, keep_down, group):
                first = pl.multiple_of((e * keep_down + k) * size, group * size)
                term = contract_last(left, dw_ref[pl.ds(first, group * size), :])
                for q in range(group):
                    h = down_index[e * keep_down + k + q]
                    grad_hidden[h] += term[:, q * size : (q + 1) * size]
        return carry

    lax.fori_loop(0, width_blocks // DOWN_UNROLL, down_step, 0)
    part = 3

    def up_step(step, carry):
        for cc in range(UP_UNROLL):
            c = step * UP_UNROLL + cc
            left = (slope_ref[c] * grad_hidden[c]).astype(BF16)
            for k in range(0, keep_up, part):
                first = pl.multiple_of((c * keep_up + k) * size, part * size)
                term = contract_last(left, uw_ref[pl.ds(first, part * size), :])
                for q in range(part):
                    w = up_index[c * keep_up + k + q]
                    grad_normed[w] += term[:, q * size : (q + 1) * size]
        return carry

    lax.fori_loop(0, hidden_blocks // UP_UNROLL, up_step, 0)
    x = x_ref[...].astype(F32)
    features = x.shape[1]
    inverse = lax.rsqrt(jnp.mean(x * x, axis=-1, keepdims=True) + EPSILON)
    along = jnp.zeros((x.shape[0], size), F32)
    for b in range(width_blocks):
        cols = slice(b * size, (b + 1) * size)
        scaled = grad_normed[b] * s_ref[:, cols]
        grad_normed[b] = scaled
        along += scaled * x_ref[:, cols].astype(F32)
    mean = jnp.sum(along, axis=-1, keepdims=True) * (1.0 / features)
    factor = inverse * inverse * inverse * mean
    for b in range(width_blocks):
        cols = slice(b * size, (b + 1) * size)
        grad = inverse * grad_normed[b] - x_ref[:, cols].astype(F32) * factor
        out_ref[:, cols] = (cot_ref[:, cols].astype(F32) + grad).astype(BF16)


def section_backward(turn, first_turn, states, stream, scale_plus, slope, weights, indices):
    rows, features = stream.shape
    size = weights[0].shape[1]
    hidden_blocks, keep_up = indices[0].shape
    width_blocks, keep_down = indices[1].shape

    def body(*refs):
        backward_kernel(keep_up, keep_down, turn, first_turn, *refs)

    result = jax.ShapeDtypeStruct((rows, features), BF16)
    out_shape = [result] if first_turn else [result, result]
    in_specs = [SMEM, SMEM] + ([VMEM] if first_turn else [SMEM, VMEM, VMEM]) + [VMEM] * 5
    return pl.pallas_call(
        body,
        out_shape=out_shape,
        in_specs=in_specs,
        out_specs=[VMEM] * len(out_shape),
        scratch_shapes=[
            pltpu.VMEM((hidden_blocks, rows, size), F32),
            pltpu.VMEM((width_blocks, rows, size), F32),
        ],
        compiler_params=pltpu.CompilerParams(vmem_limit_bytes=LIMIT),
        cost_estimate=pl.CostEstimate(
            flops=30000000000 if turn == 1 else 1000000, bytes_accessed=100000, transcendentals=0
        ),
        name=f"backward_{turn}",
    )(*[index.reshape(-1) for index in indices], *states, stream, scale_plus, slope, *weights)


def join_kernel(own_ref, after_ref, before_ref, low_ref, high_ref, out_ref):
    rows = own_ref.shape[-1]
    half = low_ref.shape[0]

    def step(h, carry):
        for first, far_ref in ((0, low_ref), (half, high_ref)):
            at = first + h
            for i, piece in enumerate((own_ref[at], after_ref[at], before_ref[at], far_ref[h])):
                out_ref[at, :, i * rows : (i + 1) * rows] = piece
        return carry

    lax.fori_loop(0, half, step, 0)


def join_pieces(pieces):
    blocks, size, rows = pieces[0].shape
    return pl.pallas_call(
        join_kernel,
        out_shape=jax.ShapeDtypeStruct((blocks, size, ROWS * rows), pieces[0].dtype),
        in_specs=[VMEM] * len(pieces),
        out_specs=VMEM,
        compiler_params=pltpu.CompilerParams(vmem_limit_bytes=LIMIT),
        cost_estimate=pl.CostEstimate(
            flops=1000000, bytes_accessed=8 * pieces[0].size, transcendentals=0
        ),
        name="join_pieces",
    )(*pieces)


def weight_kernel(keep_down, columns, place, down_index, *refs):
    joined_ref, cot_ref, keep_ref, give_ref, block_sum, largest = refs
    size = cot_ref.shape[1] // columns
    chunk = block_sum.shape[0] // CORES
    blocks = block_sum.shape[0] // size
    far = pl.program_id(0)
    y, z, core = place[0], place[1], place[2]
    chips = pl.num_programs(0)
    owner = y * chips + lax.rem(z + far, chips)

    @pl.when(far == 0)
    def _():
        largest[...] = jnp.zeros_like(largest)

    top = largest[...]
    for g in range(blocks):
        b = owner * blocks + g
        e = lax.div(b, keep_down) - y * columns
        h = down_index[b]
        term = jnp.dot(joined_ref[h], cot_ref[:, lane_block(e, size)], preferred_element_type=F32)
        block_sum[g * size : (g + 1) * size, :] = term
        top = jnp.maximum(top, jnp.max(jnp.abs(term).reshape(-1, 8, size), axis=0))
    largest[...] = top
    rows = pl.ds(pl.multiple_of(far * chunk, 8), chunk)
    keep_ref[rows, :] = block_sum[pl.ds(pl.multiple_of(core * chunk, 8), chunk), :]
    give_ref[rows, :] = block_sum[pl.ds(pl.multiple_of((1 - core) * chunk, 8), chunk), :]

    @pl.when(far == chips - 1)
    def _():
        peak = jnp.broadcast_to(jnp.max(top), (8, size))
        keep_ref[chips * chunk :, :] = peak
        give_ref[chips * chunk :, :] = peak


def weight_gradient(joined, cot, down_index, place, chips, owners):
    size = joined.shape[1]
    width_blocks, keep_down = down_index.shape
    columns = cot.shape[1] // size
    total_rows = width_blocks * keep_down * size
    chunk = split_range(total_rows, owners)

    def body(*refs):
        weight_kernel(keep_down, columns, *refs)

    shape = jax.ShapeDtypeStruct((chips * chunk + 8, size), F32)
    return pl.pallas_call(
        body,
        out_shape=[shape, shape],
        grid_spec=pltpu.PrefetchScalarGridSpec(
            num_scalar_prefetch=2,
            grid=(chips,),
            in_specs=[
                pl.BlockSpec(joined.shape, lambda i, *_: (0, 0, 0), pipeline_mode=pl.Buffered(1)),
                pl.BlockSpec(cot.shape, whole),
            ],
            out_specs=[pl.BlockSpec(shape.shape, whole)] * 2,
            scratch_shapes=[
                pltpu.VMEM((CORES * chunk, size), F32),
                pltpu.VMEM((8, size), F32),
            ],
        ),
        compiler_params=pltpu.CompilerParams(
            dimension_semantics=("arbitrary",), vmem_limit_bytes=40 << 20
        ),
        cost_estimate=pl.CostEstimate(
            flops=2 * cot.shape[0] * chips * CORES * chunk * size,
            bytes_accessed=2 * joined.size,
            transcendentals=0,
        ),
        name="weight_gradient",
    )(place, down_index.reshape(-1), joined, cot)


def dp_route(rows, chips, move):
    owners = rows * chips * CORES
    route = []
    for source in range(owners):
        y, rest = divmod(source, chips * CORES)
        z, core = divmod(rest, CORES)
        y, z, core = move(y, z, core)
        route.append((source, (y % rows * chips + z % chips) * CORES + core % CORES))
    return route


def hidden_pieces(turned, rows, chips):
    assert rows == ROWS
    half = turned.shape[0] // 2
    down = dp_route(rows, chips, lambda y, z, core: (y - 1, z, core))
    up = dp_route(rows, chips, lambda y, z, core: (y + 1, z, core))
    after = lax.ppermute(turned, "dp", down)
    before = lax.ppermute(turned, "dp", up)
    low = lax.ppermute(after[:half], "dp", down)
    high = lax.ppermute(before[half:], "dp", up)
    return [turned, after, before, low, high]


def reduce_weight_gradient(joined, cot, down_index, rows, chips):
    owners = rows * chips * CORES
    number = lax.axis_index("dp")
    y = lax.div(number, chips * CORES)
    place = jnp.stack([y, lax.rem(lax.div(number, CORES), chips), lax.rem(number, CORES)])
    columns = split_range(cot.shape[1], rows)
    received = []
    for r in (0, 1, rows - 1, 2):
        first = lax.rem(y + rows - r, rows) * columns
        part = lax.dynamic_slice_in_dim(cot, first, columns, 1)
        if r:
            route = dp_route(rows, chips, lambda y, z, core: (y - r, z, core))
            part = lax.ppermute(part, "dp", route)
        received.append(part)
    keep, give = weight_gradient(
        joined, jnp.concatenate(received, axis=0), down_index, place, chips, owners
    )
    swap = dp_route(rows, chips, lambda y, z, core: (y, z, core + 1))
    total = keep + lax.ppermute(give, "dp", swap)
    chunk = split_range(keep.shape[0] - 8, chips)
    bound = jnp.maximum(total[chips * chunk : chips * chunk + 1], 1e-30)
    power = jnp.floor(13.0 - jnp.log2(bound))
    factor = jnp.exp2(power)
    tag = jnp.broadcast_to(power, (16, power.shape[1])).astype(F16)
    result = total[:chunk]
    for r in range(1, chips):
        coded = (total[r * chunk : (r + 1) * chunk] * factor).astype(F16)
        route = dp_route(rows, chips, lambda y, z, core: (y, z + r, core))
        got = lax.ppermute(jnp.concatenate([coded, tag], axis=0), "dp", route)
        got = got.astype(F32)
        result = result + got[:chunk] * jnp.exp2(-got[chunk : chunk + 1])
    return result


def lookup(step_values, table):
    rows = step_values.shape[0]
    result = jnp.broadcast_to(table[0][None, :], (rows, table.shape[1]))
    for i in range(1, table.shape[0]):
        result = jnp.where((step_values == i)[:, None], table[i][None, :], result)
    return result


def per_device(
    clean_latent,
    noise_latent,
    teacher_velocity,
    step_index,
    modulation,
    up_weight,
    up_rows,
    down_weight,
    down_rows,
):
    section_count = lax.axis_size("section")
    section_number = lax.axis_index("section")
    owner_count = lax.axis_size("dp")
    row_total, feature_count = clean_latent.shape
    size = up_weight.shape[2]
    loss_scale = 1.0 / math.sqrt(row_total * owner_count)
    up_flat = lax.all_gather(up_weight, "dp", axis=1, tiled=True)[0]
    up_index = up_rows[0]
    down_flat = down_weight[0]
    down_index = down_rows[0]
    table = modulation[0]
    fraction = (step_index.astype(F32) + 1.0) / table.shape[0]
    entry = (
        (1.0 - fraction)[:, None] * clean_latent.astype(F32)
        + fraction[:, None] * noise_latent.astype(F32)
    ).astype(BF16)
    scale_plus = 1.0 + lookup(step_index, table)
    indices = (up_index, down_index)
    section = section_number.reshape(1).astype(jnp.int32)
    section, entry = lax.optimization_barrier((section, entry))

    result, *weights = section_forward(
        0, False, loss_scale, (entry,), scale_plus, (up_flat, down_flat), indices, None
    )
    mine = entry
    for turn in range(1, section_count):
        last = turn == section_count - 1
        arrived = lax.ppermute(result, "section", [(turn - 1, turn)])
        result, mine, *kept = section_forward(
            turn, last, loss_scale, (section, arrived, mine), scale_plus, weights, indices,
            teacher_velocity,
        )
    slope, turned = kept
    cotangent = result
    rows = split_range(owner_count, CHIPS * CORES)
    pieces = hidden_pieces(turned, rows, CHIPS)
    states = (cotangent,)
    for turn in range(section_count - 1, 0, -1):
        first_turn = turn == section_count - 1
        sent, *moved = section_backward(
            turn, first_turn, states, mine, scale_plus, slope, weights, indices
        )
        if not first_turn:
            (cotangent,) = moved
        arrived = lax.ppermute(sent, "section", [(turn, turn - 1)])
        states = (section, arrived, cotangent)
    joined, arrived = lax.optimization_barrier((join_pieces(pieces), arrived))
    cotangent = jnp.where(section_number == 0, arrived, cotangent)

    return reduce_weight_gradient(joined, cotangent, down_index, rows, CHIPS)[None]


def solution(mesh):
    in_specs = (
        P("dp", None),
        P("dp", None),
        P("dp", None),
        P("dp"),
        P("section", None, None),
        P("section", "dp", None),
        P("section", None, None),
        P("section", None, None),
        P("section", None, None),
    )
    out_specs = P("section", "dp", None)
    return jax.shard_map(
        per_device, mesh=mesh, in_specs=in_specs, out_specs=out_specs, check_vma=False
    )
```

```python
import math

import jax
import jax.numpy as jnp
from jax import lax
from jax.experimental import pallas as pl
from jax.experimental.pallas import tpu as pltpu
from jax.sharding import PartitionSpec as P

EPSILON = 1e-06
F32 = jnp.float32
BF16 = jnp.bfloat16
F16 = jnp.float16
CORES = 2
CHIPS = 8
ORDER = (0, 1, 3, 7, 5, 4, 2, 6)
TAG = 16
UP_UNROLL = 4
DOWN_UNROLL = 3
LIMIT = 12 << 20
PARTS = 4
ROWS = 4
GELU_A = math.sqrt(2.0 / math.pi)
GELU_B = 0.044715


def lane_block(index, size):
    return pl.ds(pl.multiple_of(index * size, size), size)


def split_range(total, parts):
    assert total % parts == 0
    return total // parts


def gelu_parts(v):
    squared = v * v
    t = jnp.tanh(v * (GELU_A + (GELU_A * GELU_B) * squared))
    half = 0.5 * (1.0 + t)
    slope = half + (0.5 * v) * (1.0 - t * t) * (GELU_A + (3.0 * GELU_A * GELU_B) * squared)
    return v * half, slope


def pick(take, arrived_ref, held_ref, out_ref):
    @pl.when(take)
    def _():
        out_ref[...] = arrived_ref[...]

    @pl.when(jnp.logical_not(take))
    def _():
        out_ref[...] = held_ref[...]


def forward_kernel(keep_up, keep_down, turn, last, loss_scale, *refs):
    refs = list(refs)
    up_index, down_index = refs[:2]
    del refs[:2]
    if turn:
        section, arrived_ref, held_ref = refs[:3]
        del refs[:3]
    else:
        x_ref = refs.pop(0)
    s_ref, uw_ref, dw_ref = refs[:3]
    del refs[:3]
    if last:
        teacher_ref = refs.pop(0)
    out_ref = refs.pop(0)
    if turn:
        x_ref = refs.pop(0)
        pick(section[0] == turn, arrived_ref, held_ref, x_ref)
    copies = []
    if last:
        slope_ref, turned_ref, normed, hidden = refs
    elif turn:
        normed, hidden = refs
    else:
        uw_to, dw_to, normed, hidden, arrival = refs
        for source, target in ((uw_ref, uw_to), (dw_ref, dw_to)):
            rows = source.shape[0] // PARTS
            for p in range(PARTS):
                span = pl.ds(p * rows, rows)
                copy = pltpu.make_async_copy(
                    source.at[span, :], target.at[span, :], arrival.at[len(copies)]
                )
                copies.append(copy)
        for copy in copies[:PARTS]:
            copy.start()
        uw_ref, dw_ref = uw_to, dw_to
    size = normed.shape[-1]
    width_blocks = normed.shape[0]
    hidden_blocks = hidden.shape[0]
    x = x_ref[...].astype(F32)
    inverse = lax.rsqrt(jnp.mean(x * x, axis=-1, keepdims=True) + EPSILON)
    for b in range(width_blocks):
        cols = slice(b * size, (b + 1) * size)
        piece = x_ref[:, cols].astype(F32)
        normed[b] = (piece * inverse * s_ref[:, cols]).astype(BF16)

    rows = keep_up * size

    def up_step(step, carry):
        for cc in range(UP_UNROLL):
            c = step * UP_UNROLL + cc
            left = jnp.concatenate(
                [normed[up_index[c * keep_up + k]] for k in range(keep_up)], axis=1
            )
            first = pl.multiple_of(c * rows, rows)
            pre = jnp.dot(left, uw_ref[pl.ds(first, rows), :], preferred_element_type=F32)
            act, slope = gelu_parts(pre)
            act = act.astype(BF16)
            hidden[c] = act
            if last:
                slope_ref[c] = slope
                turned_ref[c] = act.T
        return carry

    group = 4

    def down_step(step, carry):
        for ee in range(DOWN_UNROLL):
            e = step * DOWN_UNROLL + ee
            acc = x_ref[:, lane_block(e, size)].astype(F32)
            for k in range(0, keep_down, group):
                left = jnp.concatenate(
                    [hidden[down_index[e * keep_down + k + q]] for q in range(group)], axis=1
                )
                first = pl.multiple_of((e * keep_down + k) * size, group * size)
                acc = acc + jnp.dot(
                    left, dw_ref[pl.ds(first, group * size), :], preferred_element_type=F32
                )
            result = acc.astype(BF16)
            if last:
                target = teacher_ref[:, lane_block(e, size)].astype(F32)
                result = ((result.astype(F32) - target) * loss_scale).astype(BF16)
            out_ref[:, lane_block(e, size)] = result
        return carry

    for step_of, count, waits in (
        (up_step, hidden_blocks // UP_UNROLL, copies[:PARTS]),
        (down_step, width_blocks // DOWN_UNROLL, copies[PARTS:]),
    ):
        if waits:
            per = split_range(count, PARTS)
            for p, copy in enumerate(waits):
                copy.wait()
                if step_of is up_step:
                    copies[PARTS + p].start()
                lax.fori_loop(p * per, (p + 1) * per, step_of, 0)
        else:
            lax.fori_loop(0, count, step_of, 0)


def whole(i, *_):
    return (0, 0)


SMEM = pl.BlockSpec(memory_space=pltpu.SMEM)
VMEM = pl.BlockSpec(memory_space=pltpu.VMEM)


def section_forward(turn, last, loss_scale, states, scale_plus, weights, indices, teacher):
    rows, features = scale_plus.shape
    size = weights[0].shape[1]
    hidden_blocks, keep_up = indices[0].shape
    width_blocks, keep_down = indices[1].shape
    stream = jax.ShapeDtypeStruct((rows, features), BF16)
    out_shape = [stream]
    scratch = [pltpu.VMEM((width_blocks, rows, size), BF16)]
    hidden = (hidden_blocks, rows, size)
    operands = [index.reshape(-1) for index in indices] + list(states)
    operands += [scale_plus, *weights]
    in_specs = [SMEM, SMEM] + ([SMEM, VMEM, VMEM] if turn else [VMEM]) + [VMEM]
    in_specs += [VMEM, VMEM] if turn else [pl.BlockSpec(memory_space=pltpu.HBM)] * 2
    if last:
        operands.append(teacher)
        in_specs.append(VMEM)
    if turn:
        out_shape.append(stream)
    if last:
        turned = (hidden_blocks, size, rows)
        out_shape += [jax.ShapeDtypeStruct(hidden, F32), jax.ShapeDtypeStruct(turned, BF16)]
    scratch.append(pltpu.VMEM(hidden, BF16))
    if not turn:
        out_shape += [jax.ShapeDtypeStruct(w.shape, w.dtype) for w in weights]
        scratch.append(pltpu.SemaphoreType.DMA((2 * PARTS,)))

    def body(*refs):
        forward_kernel(keep_up, keep_down, turn, last, loss_scale, *refs)

    return pl.pallas_call(
        body,
        out_shape=out_shape,
        in_specs=in_specs,
        out_specs=[VMEM] * len(out_shape),
        scratch_shapes=scratch,
        compiler_params=pltpu.CompilerParams(vmem_limit_bytes=LIMIT if turn else 31 << 20),
        cost_estimate=pl.CostEstimate(
            flops=4 * rows * weights[0].size, bytes_accessed=4 * features, transcendentals=0
        ),
        name=f"forward_{turn}",
    )(*operands)


def contract_last(left, right):
    return lax.dot_general(left, right, (((1,), (1,)), ((), ())), preferred_element_type=F32)


def backward_kernel(
    keep_up, keep_down, turn, first_turn, up_index, down_index, *refs
):
    if first_turn:
        cot_ref, x_ref, s_ref, slope_ref, uw_ref, dw_ref, out_ref, grad_hidden, grad_normed = refs
    else:
        section, arrived_ref, held_ref, *refs = refs
        x_ref, s_ref, slope_ref, uw_ref, dw_ref, out_ref, cot_ref, grad_hidden, grad_normed = refs
        pick(section[0] == turn, arrived_ref, held_ref, cot_ref)
    size = grad_hidden.shape[-1]
    width_blocks = grad_normed.shape[0]
    hidden_blocks = grad_hidden.shape[0]
    grad_hidden[...] = jnp.zeros_like(grad_hidden)
    grad_normed[...] = jnp.zeros_like(grad_normed)
    group = 4

    def down_step(step, carry):
        for ee in range(DOWN_UNROLL):
            e = step * DOWN_UNROLL + ee
            left = cot_ref[:, lane_block(e, size)]
            for k in range(0, keep_down, group):
                first = pl.multiple_of((e * keep_down + k) * size, group * size)
                term = contract_last(left, dw_ref[pl.ds(first, group * size), :])
                for q in range(group):
                    h = down_index[e * keep_down + k + q]
                    grad_hidden[h] += term[:, q * size : (q + 1) * size]
        return carry

    lax.fori_loop(0, width_blocks // DOWN_UNROLL, down_step, 0)
    part = 3

    def up_step(step, carry):
        for cc in range(UP_UNROLL):
            c = step * UP_UNROLL + cc
            left = (slope_ref[c] * grad_hidden[c]).astype(BF16)
            for k in range(0, keep_up, part):
                first = pl.multiple_of((c * keep_up + k) * size, part * size)
                term = contract_last(left, uw_ref[pl.ds(first, part * size), :])
                for q in range(part):
                    w = up_index[c * keep_up + k + q]
                    grad_normed[w] += term[:, q * size : (q + 1) * size]
        return carry

    lax.fori_loop(0, hidden_blocks // UP_UNROLL, up_step, 0)
    x = x_ref[...].astype(F32)
    features = x.shape[1]
    inverse = lax.rsqrt(jnp.mean(x * x, axis=-1, keepdims=True) + EPSILON)
    along = jnp.zeros((x.shape[0], size), F32)
    for b in range(width_blocks):
        cols = slice(b * size, (b + 1) * size)
        scaled = grad_normed[b] * s_ref[:, cols]
        grad_normed[b] = scaled
        along += scaled * x_ref[:, cols].astype(F32)
    mean = jnp.sum(along, axis=-1, keepdims=True) * (1.0 / features)
    factor = inverse * inverse * inverse * mean
    for b in range(width_blocks):
        cols = slice(b * size, (b + 1) * size)
        grad = inverse * grad_normed[b] - x_ref[:, cols].astype(F32) * factor
        out_ref[:, cols] = (cot_ref[:, cols].astype(F32) + grad).astype(BF16)


def section_backward(turn, first_turn, states, stream, scale_plus, slope, weights, indices):
    rows, features = stream.shape
    size = weights[0].shape[1]
    hidden_blocks, keep_up = indices[0].shape
    width_blocks, keep_down = indices[1].shape

    def body(*refs):
        backward_kernel(keep_up, keep_down, turn, first_turn, *refs)

    result = jax.ShapeDtypeStruct((rows, features), BF16)
    out_shape = [result] if first_turn else [result, result]
    in_specs = [SMEM, SMEM] + ([VMEM] if first_turn else [SMEM, VMEM, VMEM]) + [VMEM] * 5
    return pl.pallas_call(
        body,
        out_shape=out_shape,
        in_specs=in_specs,
        out_specs=[VMEM] * len(out_shape),
        scratch_shapes=[
            pltpu.VMEM((hidden_blocks, rows, size), F32),
            pltpu.VMEM((width_blocks, rows, size), F32),
        ],
        compiler_params=pltpu.CompilerParams(vmem_limit_bytes=LIMIT),
        cost_estimate=pl.CostEstimate(
            flops=30000000000 if turn == 1 else 1000000, bytes_accessed=100000, transcendentals=0
        ),
        name=f"backward_{turn}",
    )(*[index.reshape(-1) for index in indices], *states, stream, scale_plus, slope, *weights)


def join_kernel(own_ref, after_ref, before_ref, low_ref, high_ref, out_ref):
    rows = own_ref.shape[-1]
    half = low_ref.shape[0]

    def step(h, carry):
        for first, far_ref in ((0, low_ref), (half, high_ref)):
            at = first + h
            for i, piece in enumerate((own_ref[at], after_ref[at], before_ref[at], far_ref[h])):
                out_ref[at, :, i * rows : (i + 1) * rows] = piece
        return carry

    lax.fori_loop(0, half, step, 0)


def join_pieces(pieces):
    blocks, size, rows = pieces[0].shape
    return pl.pallas_call(
        join_kernel,
        out_shape=jax.ShapeDtypeStruct((blocks, size, ROWS * rows), pieces[0].dtype),
        in_specs=[VMEM] * len(pieces),
        out_specs=VMEM,
        compiler_params=pltpu.CompilerParams(vmem_limit_bytes=LIMIT),
        cost_estimate=pl.CostEstimate(
            flops=1000000, bytes_accessed=8 * pieces[0].size, transcendentals=0
        ),
        name="join_pieces",
    )(*pieces)


def weight_kernel(keep_down, columns, place, down_index, *refs):
    joined_ref, cot_ref, keep_ref, give_ref, block_sum, largest = refs
    size = cot_ref.shape[1] // columns
    chunk = block_sum.shape[0] // CORES
    blocks = block_sum.shape[0] // size
    far = pl.program_id(0)
    y, z, core = place[0], place[1], place[2]
    chips = pl.num_programs(0)
    owner = y * chips + lax.rem(z + place[3 + far], chips)

    @pl.when(far == 0)
    def _():
        largest[...] = jnp.zeros_like(largest)

    top = largest[...]
    for g in range(blocks):
        b = owner * blocks + g
        e = lax.div(b, keep_down) - y * columns
        h = down_index[b]
        term = jnp.dot(joined_ref[h], cot_ref[:, lane_block(e, size)], preferred_element_type=F32)
        block_sum[g * size : (g + 1) * size, :] = term
        top = jnp.maximum(top, jnp.max(jnp.abs(term).reshape(-1, 8, size), axis=0))
    largest[...] = top
    rows = pl.ds(pl.multiple_of(far * chunk, 8), chunk)
    keep_ref[rows, :] = block_sum[pl.ds(pl.multiple_of(core * chunk, 8), chunk), :]
    give_ref[rows, :] = block_sum[pl.ds(pl.multiple_of((1 - core) * chunk, 8), chunk), :]

    @pl.when(far == chips - 1)
    def _():
        peak = jnp.broadcast_to(jnp.max(top), (8, size))
        keep_ref[chips * chunk :, :] = peak
        give_ref[chips * chunk :, :] = peak


def weight_gradient(joined, cot, down_index, place, chips, owners):
    size = joined.shape[1]
    width_blocks, keep_down = down_index.shape
    columns = cot.shape[1] // size
    total_rows = width_blocks * keep_down * size
    chunk = split_range(total_rows, owners)

    def body(*refs):
        weight_kernel(keep_down, columns, *refs)

    shape = jax.ShapeDtypeStruct((chips * chunk + 8, size), F32)
    return pl.pallas_call(
        body,
        out_shape=[shape, shape],
        grid_spec=pltpu.PrefetchScalarGridSpec(
            num_scalar_prefetch=2,
            grid=(chips,),
            in_specs=[
                pl.BlockSpec(joined.shape, lambda i, *_: (0, 0, 0), pipeline_mode=pl.Buffered(1)),
                pl.BlockSpec(cot.shape, whole),
            ],
            out_specs=[pl.BlockSpec(shape.shape, whole)] * 2,
            scratch_shapes=[
                pltpu.VMEM((CORES * chunk, size), F32),
                pltpu.VMEM((8, size), F32),
            ],
        ),
        compiler_params=pltpu.CompilerParams(
            dimension_semantics=("arbitrary",), vmem_limit_bytes=40 << 20
        ),
        cost_estimate=pl.CostEstimate(
            flops=2 * cot.shape[0] * chips * CORES * chunk * size,
            bytes_accessed=2 * joined.size,
            transcendentals=0,
        ),
        name="weight_gradient",
    )(place, down_index.reshape(-1), joined, cot)


def dp_route(rows, chips, move):
    owners = rows * chips * CORES
    route = []
    for source in range(owners):
        y, rest = divmod(source, chips * CORES)
        z, core = divmod(rest, CORES)
        y, z, core = move(y, z, core)
        route.append((source, (y % rows * chips + z % chips) * CORES + core % CORES))
    return route


def hidden_pieces(turned, rows, chips):
    assert rows == ROWS and chips == CHIPS == len(ORDER)
    half = turned.shape[0] // 2
    down = dp_route(rows, chips, lambda y, z, core: (y - 1, z, core))
    up = dp_route(rows, chips, lambda y, z, core: (y + 1, z, core))
    after = lax.ppermute(turned, "dp", down)
    before = lax.ppermute(turned, "dp", up)
    low = lax.ppermute(after[:half], "dp", down)
    high = lax.ppermute(before[half:], "dp", up)
    return [turned, after, before, low, high]


def reduce_weight_gradient(joined, cot, down_index, rows, chips):
    owners = rows * chips * CORES
    number = lax.axis_index("dp")
    y = lax.div(number, chips * CORES)
    z = lax.rem(lax.div(number, CORES), chips)
    place = jnp.stack([y, z, lax.rem(number, CORES)] + [jnp.int32(far) for far in ORDER])
    columns = split_range(cot.shape[1], rows)
    received = []
    for r in (0, 1, rows - 1, 2):
        first = lax.rem(y + rows - r, rows) * columns
        part = lax.dynamic_slice_in_dim(cot, first, columns, 1)
        if r:
            route = dp_route(rows, chips, lambda y, z, core: (y - r, z, core))
            part = lax.ppermute(part, "dp", route)
        received.append(part)
    keep, give = weight_gradient(
        joined, jnp.concatenate(received, axis=0), down_index, place, chips, owners
    )
    swap = dp_route(rows, chips, lambda y, z, core: (y, z, core + 1))
    total = keep + lax.ppermute(give, "dp", swap)
    chunk = split_range(keep.shape[0] - 8, chips)
    bound = jnp.maximum(total[chips * chunk : chips * chunk + 1], 1e-30)
    power = jnp.floor(13.0 - jnp.log2(bound))

    def send(values, power, steps):
        tag = jnp.broadcast_to(power, (TAG, power.shape[1]))
        coded = jnp.concatenate([values * jnp.exp2(power), tag], axis=0).astype(F16)
        route = dp_route(rows, chips, lambda y, z, core: (y, z + steps, core))
        got = lax.ppermute(coded, "dp", route).astype(F32)
        power = got[-TAG : 1 - TAG]
        return got[:-TAG] * jnp.exp2(-power), power

    half = chunk // 2
    middle = 5 * chunk
    from_below, power_below = send(total[chunk : 3 * chunk], power, 1)
    from_above, power_above = send(total[3 * chunk : middle], power, -1)
    low, power_low = send(total[middle : middle + half], power, 2)
    high, power_high = send(total[middle + half : middle + chunk], power, -2)
    upward = total[6 * chunk : 7 * chunk] + from_below[chunk:]
    upward = jnp.concatenate([upward[:half] + low, upward[half:]], axis=0)
    downward = total[7 * chunk : 8 * chunk] + from_above[chunk:]
    downward = jnp.concatenate([downward[:half], downward[half:] + high], axis=0)
    up_power = jnp.minimum(jnp.minimum(power, power_below), power_low) - 2.0
    down_power = jnp.minimum(jnp.minimum(power, power_above), power_high) - 2.0
    result = total[:chunk] + from_below[:chunk] + from_above[:chunk]
    result = result + send(upward, up_power, 2)[0]
    return result + send(downward, down_power, -2)[0]


def lookup(step_values, table):
    rows = step_values.shape[0]
    result = jnp.broadcast_to(table[0][None, :], (rows, table.shape[1]))
    for i in range(1, table.shape[0]):
        result = jnp.where((step_values == i)[:, None], table[i][None, :], result)
    return result


def per_device(
    clean_latent,
    noise_latent,
    teacher_velocity,
    step_index,
    modulation,
    up_weight,
    up_rows,
    down_weight,
    down_rows,
):
    section_count = lax.axis_size("section")
    section_number = lax.axis_index("section")
    owner_count = lax.axis_size("dp")
    row_total, feature_count = clean_latent.shape
    size = up_weight.shape[2]
    loss_scale = 1.0 / math.sqrt(row_total * owner_count)
    up_flat = lax.all_gather(up_weight, "dp", axis=1, tiled=True)[0]
    up_index = up_rows[0]
    down_flat = down_weight[0]
    down_index = down_rows[0]
    table = modulation[0]
    fraction = (step_index.astype(F32) + 1.0) / table.shape[0]
    entry = (
        (1.0 - fraction)[:, None] * clean_latent.astype(F32)
        + fraction[:, None] * noise_latent.astype(F32)
    ).astype(BF16)
    scale_plus = 1.0 + lookup(step_index, table)
    indices = (up_index, down_index)
    section = section_number.reshape(1).astype(jnp.int32)
    section, entry = lax.optimization_barrier((section, entry))

    result, *weights = section_forward(
        0, False, loss_scale, (entry,), scale_plus, (up_flat, down_flat), indices, None
    )
    mine = entry
    for turn in range(1, section_count):
        last = turn == section_count - 1
        arrived = lax.ppermute(result, "section", [(turn - 1, turn)])
        result, mine, *kept = section_forward(
            turn, last, loss_scale, (section, arrived, mine), scale_plus, weights, indices,
            teacher_velocity,
        )
    slope, turned = kept
    cotangent = result
    rows = split_range(owner_count, CHIPS * CORES)
    pieces = hidden_pieces(turned, rows, CHIPS)
    states = (cotangent,)
    for turn in range(section_count - 1, 0, -1):
        first_turn = turn == section_count - 1
        sent, *moved = section_backward(
            turn, first_turn, states, mine, scale_plus, slope, weights, indices
        )
        if not first_turn:
            (cotangent,) = moved
        arrived = lax.ppermute(sent, "section", [(turn, turn - 1)])
        states = (section, arrived, cotangent)
    joined, arrived = lax.optimization_barrier((join_pieces(pieces), arrived))
    cotangent = jnp.where(section_number == 0, arrived, cotangent)

    return reduce_weight_gradient(joined, cotangent, down_index, rows, CHIPS)[None]


def solution(mesh):
    in_specs = (
        P("dp", None),
        P("dp", None),
        P("dp", None),
        P("dp"),
        P("section", None, None),
        P("section", "dp", None),
        P("section", None, None),
        P("section", None, None),
        P("section", None, None),
    )
    out_specs = P("section", "dp", None)
    return jax.shard_map(
        per_device, mesh=mesh, in_specs=in_specs, out_specs=out_specs, check_vma=False
    )
```

```python
import math

import jax
import jax.numpy as jnp
from jax import lax
from jax.experimental import pallas as pl
from jax.experimental.pallas import tpu as pltpu
from jax.sharding import PartitionSpec as P

EPSILON = 1e-06
F32 = jnp.float32
BF16 = jnp.bfloat16
F16 = jnp.float16
CORES = 2
CHIPS = 8
ORDER = (0, 1, 3, 7, 5, 4, 2, 6)
TAG = 16
FORWARD_GROUP = 4
DOWN_GROUP = 12
UP_GROUP = 6
UP_UNROLL = 16
DOWN_UNROLL = 6
FORWARD_UNROLL = 12
FORWARD_DOWN = 3
LIMIT = 12 << 20
PARTS = 4
ROWS = 4
GELU_A = math.sqrt(2.0 / math.pi)
GELU_B = 0.044715


def lane_block(index, size):
    return pl.ds(pl.multiple_of(index * size, size), size)


def split_range(total, parts):
    assert total % parts == 0
    return total // parts


def gelu_parts(v):
    squared = v * v
    t = jnp.tanh(v * (GELU_A + (GELU_A * GELU_B) * squared))
    half = 0.5 * (1.0 + t)
    slope = half + (0.5 * v) * (1.0 - t * t) * (GELU_A + (3.0 * GELU_A * GELU_B) * squared)
    return v * half, slope


def pick(take, arrived_ref, held_ref, out_ref):
    @pl.when(take)
    def _():
        out_ref[...] = arrived_ref[...]

    @pl.when(jnp.logical_not(take))
    def _():
        out_ref[...] = held_ref[...]


def part_copy(source, target, part, semaphore):
    rows = source.shape[0] // PARTS
    first = part * rows
    span = pl.ds(first if isinstance(part, int) else pl.multiple_of(first, rows), rows)
    return pltpu.make_async_copy(source.at[span, :], target.at[span, :], semaphore)


def forward_kernel(keep_up, keep_down, turn, last, loss_scale, *refs):
    refs = list(refs)
    up_index, down_index = refs[:2]
    del refs[:2]
    if turn:
        section, arrived_ref, held_ref = refs[:3]
        del refs[:3]
    else:
        x_ref = refs.pop(0)
    s_ref, uw_ref, dw_ref = refs[:3]
    del refs[:3]
    if last:
        teacher_ref = refs.pop(0)
    out_ref = refs.pop(0)
    if turn:
        x_ref = refs.pop(0)
        pick(section[0] == turn, arrived_ref, held_ref, x_ref)
    if last:
        slope_ref, turned_ref, normed, hidden = refs
    elif turn:
        normed, hidden = refs
    else:
        uw_to, dw_to, normed, hidden, arrival = refs
        uw_from, dw_from = uw_ref, dw_ref
        uw_ref, dw_ref = uw_to, dw_to

    def up_copy(part):
        return part_copy(uw_from, uw_to, part, arrival.at[part])

    def down_copy(part):
        return part_copy(dw_from, dw_to, part, arrival.at[PARTS + part])

    if not turn:
        for part in range(PARTS):
            up_copy(part).start()
    size = normed.shape[-1]
    width_blocks = normed.shape[0]
    hidden_blocks = hidden.shape[0]
    x = x_ref[...].astype(F32)
    inverse = lax.rsqrt(jnp.mean(x * x, axis=-1, keepdims=True) + EPSILON)
    for b in range(width_blocks):
        cols = slice(b * size, (b + 1) * size)
        piece = x_ref[:, cols].astype(F32)
        normed[b] = (piece * inverse * s_ref[:, cols]).astype(BF16)

    rows = keep_up * size
    up_unroll, down_unroll = FORWARD_UNROLL, FORWARD_DOWN
    if not turn:
        up_unroll, down_unroll = hidden_blocks // PARTS, width_blocks // PARTS

    def up_step(step, carry):
        if not turn:
            up_copy(step).wait()
            down_copy(step).start()
        for cc in range(up_unroll):
            c = step * up_unroll + cc
            left = jnp.concatenate(
                [normed[up_index[c * keep_up + k]] for k in range(keep_up)], axis=1
            )
            first = pl.multiple_of(c * rows, rows)
            pre = jnp.dot(left, uw_ref[pl.ds(first, rows), :], preferred_element_type=F32)
            act, slope = gelu_parts(pre)
            act = act.astype(BF16)
            hidden[c] = act
            if last:
                slope_ref[c] = slope
                turned_ref[c] = act.T
        return carry

    group = FORWARD_GROUP

    def down_step(step, carry):
        if not turn:
            down_copy(step).wait()
        for ee in range(down_unroll):
            e = step * down_unroll + ee
            acc = x_ref[:, lane_block(e, size)].astype(F32)
            for k in range(0, keep_down, group):
                left = jnp.concatenate(
                    [hidden[down_index[e * keep_down + k + q]] for q in range(group)], axis=1
                )
                first = pl.multiple_of((e * keep_down + k) * size, group * size)
                acc = acc + jnp.dot(
                    left, dw_ref[pl.ds(first, group * size), :], preferred_element_type=F32
                )
            result = acc.astype(BF16)
            if last:
                target = teacher_ref[:, lane_block(e, size)].astype(F32)
                result = ((result.astype(F32) - target) * loss_scale).astype(BF16)
            out_ref[:, lane_block(e, size)] = result
        return carry

    lax.fori_loop(0, hidden_blocks // up_unroll, up_step, 0)
    lax.fori_loop(0, width_blocks // down_unroll, down_step, 0)


def whole(i, *_):
    return (0, 0)


SMEM = pl.BlockSpec(memory_space=pltpu.SMEM)
VMEM = pl.BlockSpec(memory_space=pltpu.VMEM)


def section_forward(turn, last, loss_scale, states, scale_plus, weights, indices, teacher):
    rows, features = scale_plus.shape
    size = weights[0].shape[1]
    hidden_blocks, keep_up = indices[0].shape
    width_blocks, keep_down = indices[1].shape
    stream = jax.ShapeDtypeStruct((rows, features), BF16)
    out_shape = [stream]
    scratch = [pltpu.VMEM((width_blocks, rows, size), BF16)]
    hidden = (hidden_blocks, rows, size)
    operands = [index.reshape(-1) for index in indices] + list(states)
    operands += [scale_plus, *weights]
    in_specs = [SMEM, SMEM] + ([SMEM, VMEM, VMEM] if turn else [VMEM]) + [VMEM]
    in_specs += [VMEM, VMEM] if turn else [pl.BlockSpec(memory_space=pltpu.HBM)] * 2
    if last:
        operands.append(teacher)
        in_specs.append(VMEM)
    if turn:
        out_shape.append(stream)
    if last:
        turned = (hidden_blocks, size, rows)
        out_shape += [jax.ShapeDtypeStruct(hidden, F32), jax.ShapeDtypeStruct(turned, BF16)]
    scratch.append(pltpu.VMEM(hidden, BF16))
    if not turn:
        out_shape += [jax.ShapeDtypeStruct(w.shape, w.dtype) for w in weights]
        scratch.append(pltpu.SemaphoreType.DMA((2 * PARTS,)))

    def body(*refs):
        forward_kernel(keep_up, keep_down, turn, last, loss_scale, *refs)

    return pl.pallas_call(
        body,
        out_shape=out_shape,
        in_specs=in_specs,
        out_specs=[VMEM] * len(out_shape),
        scratch_shapes=scratch,
        compiler_params=pltpu.CompilerParams(vmem_limit_bytes=LIMIT if turn else 31 << 20),
        cost_estimate=pl.CostEstimate(
            flops=4 * rows * weights[0].size, bytes_accessed=4 * features, transcendentals=0
        ),
        name=f"forward_{turn}",
    )(*operands)


def contract_last(left, right):
    return lax.dot_general(left, right, (((1,), (1,)), ((), ())), preferred_element_type=F32)


def backward_kernel(
    keep_up, keep_down, turn, first_turn, up_index, down_index, *refs
):
    if first_turn:
        cot_ref, x_ref, s_ref, slope_ref, uw_ref, dw_ref, out_ref, grad_hidden, grad_normed = refs
    else:
        section, arrived_ref, held_ref, *refs = refs
        x_ref, s_ref, slope_ref, uw_ref, dw_ref, out_ref, cot_ref, grad_hidden, grad_normed = refs
        pick(section[0] == turn, arrived_ref, held_ref, cot_ref)
    size = grad_hidden.shape[-1]
    width_blocks = grad_normed.shape[0]
    hidden_blocks = grad_hidden.shape[0]
    grad_hidden[...] = jnp.zeros_like(grad_hidden)
    grad_normed[...] = jnp.zeros_like(grad_normed)
    group = DOWN_GROUP

    def down_step(step, carry):
        for ee in range(DOWN_UNROLL):
            e = step * DOWN_UNROLL + ee
            left = cot_ref[:, lane_block(e, size)]
            for k in range(0, keep_down, group):
                first = pl.multiple_of((e * keep_down + k) * size, group * size)
                term = contract_last(left, dw_ref[pl.ds(first, group * size), :])
                for q in range(group):
                    h = down_index[e * keep_down + k + q]
                    grad_hidden[h] += term[:, q * size : (q + 1) * size]
        return carry

    lax.fori_loop(0, width_blocks // DOWN_UNROLL, down_step, 0)
    part = UP_GROUP

    def up_step(step, carry):
        for cc in range(UP_UNROLL):
            c = step * UP_UNROLL + cc
            left = (slope_ref[c] * grad_hidden[c]).astype(BF16)
            for k in range(0, keep_up, part):
                first = pl.multiple_of((c * keep_up + k) * size, part * size)
                term = contract_last(left, uw_ref[pl.ds(first, part * size), :])
                for q in range(part):
                    w = up_index[c * keep_up + k + q]
                    grad_normed[w] += term[:, q * size : (q + 1) * size]
        return carry

    lax.fori_loop(0, hidden_blocks // UP_UNROLL, up_step, 0)
    x = x_ref[...].astype(F32)
    features = x.shape[1]
    inverse = lax.rsqrt(jnp.mean(x * x, axis=-1, keepdims=True) + EPSILON)
    along = jnp.zeros((x.shape[0], size), F32)
    for b in range(width_blocks):
        cols = slice(b * size, (b + 1) * size)
        scaled = grad_normed[b] * s_ref[:, cols]
        grad_normed[b] = scaled
        along += scaled * x_ref[:, cols].astype(F32)
    mean = jnp.sum(along, axis=-1, keepdims=True) * (1.0 / features)
    factor = inverse * inverse * inverse * mean
    for b in range(width_blocks):
        cols = slice(b * size, (b + 1) * size)
        grad = inverse * grad_normed[b] - x_ref[:, cols].astype(F32) * factor
        out_ref[:, cols] = (cot_ref[:, cols].astype(F32) + grad).astype(BF16)


def section_backward(turn, first_turn, states, stream, scale_plus, slope, weights, indices):
    rows, features = stream.shape
    size = weights[0].shape[1]
    hidden_blocks, keep_up = indices[0].shape
    width_blocks, keep_down = indices[1].shape

    def body(*refs):
        backward_kernel(keep_up, keep_down, turn, first_turn, *refs)

    result = jax.ShapeDtypeStruct((rows, features), BF16)
    out_shape = [result] if first_turn else [result, result]
    in_specs = [SMEM, SMEM] + ([VMEM] if first_turn else [SMEM, VMEM, VMEM]) + [VMEM] * 5
    return pl.pallas_call(
        body,
        out_shape=out_shape,
        in_specs=in_specs,
        out_specs=[VMEM] * len(out_shape),
        scratch_shapes=[
            pltpu.VMEM((hidden_blocks, rows, size), F32),
            pltpu.VMEM((width_blocks, rows, size), F32),
        ],
        compiler_params=pltpu.CompilerParams(vmem_limit_bytes=LIMIT),
        cost_estimate=pl.CostEstimate(
            flops=30000000000 if turn == 1 else 1000000, bytes_accessed=100000, transcendentals=0
        ),
        name=f"backward_{turn}",
    )(*[index.reshape(-1) for index in indices], *states, stream, scale_plus, slope, *weights)


def join_kernel(own_ref, after_ref, before_ref, low_ref, high_ref, out_ref):
    rows = own_ref.shape[-1]
    half = low_ref.shape[0]

    def step(h, carry):
        for first, far_ref in ((0, low_ref), (half, high_ref)):
            at = first + h
            for i, piece in enumerate((own_ref[at], after_ref[at], before_ref[at], far_ref[h])):
                out_ref[at, :, i * rows : (i + 1) * rows] = piece
        return carry

    lax.fori_loop(0, half, step, 0)


def join_pieces(pieces):
    blocks, size, rows = pieces[0].shape
    return pl.pallas_call(
        join_kernel,
        out_shape=jax.ShapeDtypeStruct((blocks, size, ROWS * rows), pieces[0].dtype),
        in_specs=[VMEM] * len(pieces),
        out_specs=VMEM,
        compiler_params=pltpu.CompilerParams(vmem_limit_bytes=LIMIT),
        cost_estimate=pl.CostEstimate(
            flops=1000000, bytes_accessed=8 * pieces[0].size, transcendentals=0
        ),
        name="join_pieces",
    )(*pieces)


def weight_kernel(keep_down, columns, place, down_index, *refs):
    joined_ref, cot_ref, keep_ref, give_ref, block_sum, largest = refs
    size = cot_ref.shape[1] // columns
    chunk = block_sum.shape[0] // CORES
    blocks = block_sum.shape[0] // size
    far = pl.program_id(0)
    y, z, core = place[0], place[1], place[2]
    chips = pl.num_programs(0)
    owner = y * chips + lax.rem(z + place[3 + far], chips)

    @pl.when(far == 0)
    def _():
        largest[...] = jnp.zeros_like(largest)

    top = largest[...]
    for g in range(blocks):
        b = owner * blocks + g
        e = lax.div(b, keep_down) - y * columns
        h = down_index[b]
        term = jnp.dot(joined_ref[h], cot_ref[:, lane_block(e, size)], preferred_element_type=F32)
        block_sum[g * size : (g + 1) * size, :] = term
        top = jnp.maximum(top, jnp.max(jnp.abs(term).reshape(-1, 8, size), axis=0))
    largest[...] = top
    rows = pl.ds(pl.multiple_of(far * chunk, 8), chunk)
    keep_ref[rows, :] = block_sum[pl.ds(pl.multiple_of(core * chunk, 8), chunk), :]
    give_ref[rows, :] = block_sum[pl.ds(pl.multiple_of((1 - core) * chunk, 8), chunk), :]

    @pl.when(far == chips - 1)
    def _():
        peak = jnp.broadcast_to(jnp.max(top), (8, size))
        keep_ref[chips * chunk :, :] = peak
        give_ref[chips * chunk :, :] = peak


def weight_gradient(joined, cot, down_index, place, chips, owners):
    size = joined.shape[1]
    width_blocks, keep_down = down_index.shape
    columns = cot.shape[1] // size
    total_rows = width_blocks * keep_down * size
    chunk = split_range(total_rows, owners)

    def body(*refs):
        weight_kernel(keep_down, columns, *refs)

    shape = jax.ShapeDtypeStruct((chips * chunk + 8, size), F32)
    return pl.pallas_call(
        body,
        out_shape=[shape, shape],
        grid_spec=pltpu.PrefetchScalarGridSpec(
            num_scalar_prefetch=2,
            grid=(chips,),
            in_specs=[
                pl.BlockSpec(joined.shape, lambda i, *_: (0, 0, 0), pipeline_mode=pl.Buffered(1)),
                pl.BlockSpec(cot.shape, whole),
            ],
            out_specs=[pl.BlockSpec(shape.shape, whole)] * 2,
            scratch_shapes=[
                pltpu.VMEM((CORES * chunk, size), F32),
                pltpu.VMEM((8, size), F32),
            ],
        ),
        compiler_params=pltpu.CompilerParams(
            dimension_semantics=("arbitrary",), vmem_limit_bytes=40 << 20
        ),
        cost_estimate=pl.CostEstimate(
            flops=2 * cot.shape[0] * chips * CORES * chunk * size,
            bytes_accessed=2 * joined.size,
            transcendentals=0,
        ),
        name="weight_gradient",
    )(place, down_index.reshape(-1), joined, cot)


def dp_route(rows, chips, move):
    owners = rows * chips * CORES
    route = []
    for source in range(owners):
        y, rest = divmod(source, chips * CORES)
        z, core = divmod(rest, CORES)
        y, z, core = move(y, z, core)
        route.append((source, (y % rows * chips + z % chips) * CORES + core % CORES))
    return route


def hidden_pieces(turned, rows, chips):
    assert rows == ROWS and chips == CHIPS == len(ORDER)
    half = turned.shape[0] // 2
    down = dp_route(rows, chips, lambda y, z, core: (y - 1, z, core))
    up = dp_route(rows, chips, lambda y, z, core: (y + 1, z, core))
    after = lax.ppermute(turned, "dp", down)
    before = lax.ppermute(turned, "dp", up)
    low = lax.ppermute(after[:half], "dp", down)
    high = lax.ppermute(before[half:], "dp", up)
    return [turned, after, before, low, high]


def reduce_weight_gradient(joined, cot, down_index, rows, chips):
    owners = rows * chips * CORES
    number = lax.axis_index("dp")
    y = lax.div(number, chips * CORES)
    z = lax.rem(lax.div(number, CORES), chips)
    place = jnp.stack([y, z, lax.rem(number, CORES)] + [jnp.int32(far) for far in ORDER])
    columns = split_range(cot.shape[1], rows)
    received = []
    for r in (0, 1, rows - 1, 2):
        first = lax.rem(y + rows - r, rows) * columns
        part = lax.dynamic_slice_in_dim(cot, first, columns, 1)
        if r:
            route = dp_route(rows, chips, lambda y, z, core: (y - r, z, core))
            part = lax.ppermute(part, "dp", route)
        received.append(part)
    keep, give = weight_gradient(
        joined, jnp.concatenate(received, axis=0), down_index, place, chips, owners
    )
    swap = dp_route(rows, chips, lambda y, z, core: (y, z, core + 1))
    total = keep + lax.ppermute(give, "dp", swap)
    chunk = split_range(keep.shape[0] - 8, chips)
    bound = jnp.maximum(total[chips * chunk : chips * chunk + 1], 1e-30)
    power = jnp.floor(13.0 - jnp.log2(bound))

    def send(values, power, steps):
        tag = jnp.broadcast_to(power, (TAG, power.shape[1]))
        coded = jnp.concatenate([values * jnp.exp2(power), tag], axis=0).astype(F16)
        route = dp_route(rows, chips, lambda y, z, core: (y, z + steps, core))
        got = lax.ppermute(coded, "dp", route).astype(F32)
        power = got[-TAG : 1 - TAG]
        return got[:-TAG] * jnp.exp2(-power), power

    half = chunk // 2
    middle = 5 * chunk
    from_below, power_below = send(total[chunk : 3 * chunk], power, 1)
    from_above, power_above = send(total[3 * chunk : middle], power, -1)
    low, power_low = send(total[middle : middle + half], power, 2)
    high, power_high = send(total[middle + half : middle + chunk], power, -2)
    upward = total[6 * chunk : 7 * chunk] + from_below[chunk:]
    upward = jnp.concatenate([upward[:half] + low, upward[half:]], axis=0)
    downward = total[7 * chunk : 8 * chunk] + from_above[chunk:]
    downward = jnp.concatenate([downward[:half], downward[half:] + high], axis=0)
    up_power = jnp.minimum(jnp.minimum(power, power_below), power_low) - 2.0
    down_power = jnp.minimum(jnp.minimum(power, power_above), power_high) - 2.0
    result = total[:chunk] + from_below[:chunk] + from_above[:chunk]
    result = result + send(upward, up_power, 2)[0]
    return result + send(downward, down_power, -2)[0]


def lookup(step_values, table):
    rows = step_values.shape[0]
    result = jnp.broadcast_to(table[0][None, :], (rows, table.shape[1]))
    for i in range(1, table.shape[0]):
        result = jnp.where((step_values == i)[:, None], table[i][None, :], result)
    return result


def per_device(
    clean_latent,
    noise_latent,
    teacher_velocity,
    step_index,
    modulation,
    up_weight,
    up_rows,
    down_weight,
    down_rows,
):
    section_count = lax.axis_size("section")
    section_number = lax.axis_index("section")
    owner_count = lax.axis_size("dp")
    row_total, feature_count = clean_latent.shape
    size = up_weight.shape[2]
    loss_scale = 1.0 / math.sqrt(row_total * owner_count)
    up_flat = lax.all_gather(up_weight, "dp", axis=1, tiled=True)[0]
    up_index = up_rows[0]
    down_flat = down_weight[0]
    down_index = down_rows[0]
    table = modulation[0]
    fraction = (step_index.astype(F32) + 1.0) / table.shape[0]
    entry = (
        (1.0 - fraction)[:, None] * clean_latent.astype(F32)
        + fraction[:, None] * noise_latent.astype(F32)
    ).astype(BF16)
    scale_plus = 1.0 + lookup(step_index, table)
    indices = (up_index, down_index)
    section = section_number.reshape(1).astype(jnp.int32)
    section, entry = lax.optimization_barrier((section, entry))

    result, *weights = section_forward(
        0, False, loss_scale, (entry,), scale_plus, (up_flat, down_flat), indices, None
    )
    mine = entry
    for turn in range(1, section_count):
        last = turn == section_count - 1
        arrived = lax.ppermute(result, "section", [(turn - 1, turn)])
        result, mine, *kept = section_forward(
            turn, last, loss_scale, (section, arrived, mine), scale_plus, weights, indices,
            teacher_velocity,
        )
    slope, turned = kept
    cotangent = result
    rows = split_range(owner_count, CHIPS * CORES)
    pieces = hidden_pieces(turned, rows, CHIPS)
    states = (cotangent,)
    for turn in range(section_count - 1, 0, -1):
        first_turn = turn == section_count - 1
        sent, *moved = section_backward(
            turn, first_turn, states, mine, scale_plus, slope, weights, indices
        )
        if not first_turn:
            (cotangent,) = moved
        arrived = lax.ppermute(sent, "section", [(turn, turn - 1)])
        states = (section, arrived, cotangent)
    joined, arrived = lax.optimization_barrier((join_pieces(pieces), arrived))
    cotangent = jnp.where(section_number == 0, arrived, cotangent)

    return reduce_weight_gradient(joined, cotangent, down_index, rows, CHIPS)[None]


def solution(mesh):
    in_specs = (
        P("dp", None),
        P("dp", None),
        P("dp", None),
        P("dp"),
        P("section", None, None),
        P("section", "dp", None),
        P("section", None, None),
        P("section", None, None),
        P("section", None, None),
    )
    out_specs = P("section", "dp", None)
    return jax.shard_map(
        per_device, mesh=mesh, in_specs=in_specs, out_specs=out_specs, check_vma=False
    )
```

```python
import math

import jax
import jax.numpy as jnp
from jax import lax
from jax.experimental import pallas as pl
from jax.experimental.pallas import tpu as pltpu
from jax.sharding import PartitionSpec as P

EPSILON = 1e-06
F32 = jnp.float32
BF16 = jnp.bfloat16
F16 = jnp.float16
CORES = 2
CHIPS = 8
ORDER = (0, 1, 3, 7, 5, 4, 2, 6)
TAG = 16
FORWARD_GROUP = 4
DOWN_GROUP = 12
UP_GROUP = 6
UP_UNROLL = 16
DOWN_UNROLL = 3
FORWARD_UNROLL = 12
FORWARD_DOWN = 3
LIMIT = 12 << 20
PARTS = 4
ROWS = 4
GELU_A = math.sqrt(2.0 / math.pi)
GELU_B = 0.044715


def lane_block(index, size):
    return pl.ds(pl.multiple_of(index * size, size), size)


def split_range(total, parts):
    assert total % parts == 0
    return total // parts


def gelu_parts(v):
    squared = v * v
    t = jnp.tanh(v * (GELU_A + (GELU_A * GELU_B) * squared))
    half = 0.5 * (1.0 + t)
    slope = half + (0.5 * v) * (1.0 - t * t) * (GELU_A + (3.0 * GELU_A * GELU_B) * squared)
    return v * half, slope


def pick(take, arrived_ref, held_ref, out_ref):
    @pl.when(take)
    def _():
        out_ref[...] = arrived_ref[...]

    @pl.when(jnp.logical_not(take))
    def _():
        out_ref[...] = held_ref[...]


def part_copy(source, target, part, semaphore):
    rows = source.shape[0] // PARTS
    first = part * rows
    span = pl.ds(first if isinstance(part, int) else pl.multiple_of(first, rows), rows)
    return pltpu.make_async_copy(source.at[span, :], target.at[span, :], semaphore)


def forward_kernel(keep_up, keep_down, turn, last, loss_scale, *refs):
    refs = list(refs)
    up_index, down_index = refs[:2]
    del refs[:2]
    if turn:
        section, arrived_ref, held_ref = refs[:3]
        del refs[:3]
    else:
        x_ref = refs.pop(0)
    s_ref, uw_ref, dw_ref = refs[:3]
    del refs[:3]
    if last:
        teacher_ref = refs.pop(0)
    out_ref = refs.pop(0)
    if turn:
        x_ref = refs.pop(0)
        pick(section[0] == turn, arrived_ref, held_ref, x_ref)
    if last:
        slope_ref, turned_ref, normed, hidden = refs
    elif turn:
        normed, hidden = refs
    else:
        uw_to, dw_to, normed, hidden, arrival = refs
        uw_from, dw_from = uw_ref, dw_ref
        uw_ref, dw_ref = uw_to, dw_to

    def up_copy(part):
        return part_copy(uw_from, uw_to, part, arrival.at[part])

    def down_copy(part):
        return part_copy(dw_from, dw_to, part, arrival.at[PARTS + part])

    if not turn:
        for part in range(PARTS):
            up_copy(part).start()
    size = normed.shape[-1]
    width_blocks = normed.shape[0]
    hidden_blocks = hidden.shape[0]
    x = x_ref[...].astype(F32)
    inverse = lax.rsqrt(jnp.mean(x * x, axis=-1, keepdims=True) + EPSILON)
    for b in range(width_blocks):
        cols = slice(b * size, (b + 1) * size)
        piece = x_ref[:, cols].astype(F32)
        normed[b] = (piece * inverse * s_ref[:, cols]).astype(BF16)

    rows = keep_up * size
    up_unroll, down_unroll = FORWARD_UNROLL, FORWARD_DOWN
    if not turn:
        up_unroll, down_unroll = hidden_blocks // PARTS, width_blocks // PARTS

    def up_step(step, carry):
        if not turn:
            up_copy(step).wait()
            down_copy(step).start()
        for cc in range(up_unroll):
            c = step * up_unroll + cc
            left = jnp.concatenate(
                [normed[up_index[c * keep_up + k]] for k in range(keep_up)], axis=1
            )
            first = pl.multiple_of(c * rows, rows)
            pre = jnp.dot(left, uw_ref[pl.ds(first, rows), :], preferred_element_type=F32)
            act, slope = gelu_parts(pre)
            act = act.astype(BF16)
            hidden[c] = act
            if last:
                slope_ref[c] = slope
                turned_ref[c] = act.T
        return carry

    group = FORWARD_GROUP

    def down_step(step, carry):
        if not turn:
            down_copy(step).wait()
        for ee in range(down_unroll):
            e = step * down_unroll + ee
            acc = x_ref[:, lane_block(e, size)].astype(F32)
            for k in range(0, keep_down, group):
                left = jnp.concatenate(
                    [hidden[down_index[e * keep_down + k + q]] for q in range(group)], axis=1
                )
                first = pl.multiple_of((e * keep_down + k) * size, group * size)
                acc = acc + jnp.dot(
                    left, dw_ref[pl.ds(first, group * size), :], preferred_element_type=F32
                )
            result = acc.astype(BF16)
            if last:
                target = teacher_ref[:, lane_block(e, size)].astype(F32)
                result = ((result.astype(F32) - target) * loss_scale).astype(BF16)
            out_ref[:, lane_block(e, size)] = result
        return carry

    lax.fori_loop(0, hidden_blocks // up_unroll, up_step, 0)
    lax.fori_loop(0, width_blocks // down_unroll, down_step, 0)


def whole(i, *_):
    return (0, 0)


SMEM = pl.BlockSpec(memory_space=pltpu.SMEM)
VMEM = pl.BlockSpec(memory_space=pltpu.VMEM)


def section_forward(turn, last, loss_scale, states, scale_plus, weights, indices, teacher):
    rows, features = scale_plus.shape
    size = weights[0].shape[1]
    hidden_blocks, keep_up = indices[0].shape
    width_blocks, keep_down = indices[1].shape
    stream = jax.ShapeDtypeStruct((rows, features), BF16)
    out_shape = [stream]
    scratch = [pltpu.VMEM((width_blocks, rows, size), BF16)]
    hidden = (hidden_blocks, rows, size)
    operands = [index.reshape(-1) for index in indices] + list(states)
    operands += [scale_plus, *weights]
    in_specs = [SMEM, SMEM] + ([SMEM, VMEM, VMEM] if turn else [VMEM]) + [VMEM]
    in_specs += [VMEM, VMEM] if turn else [pl.BlockSpec(memory_space=pltpu.HBM)] * 2
    if last:
        operands.append(teacher)
        in_specs.append(VMEM)
    if turn:
        out_shape.append(stream)
    if last:
        turned = (hidden_blocks, size, rows)
        out_shape += [jax.ShapeDtypeStruct(hidden, F32), jax.ShapeDtypeStruct(turned, BF16)]
    scratch.append(pltpu.VMEM(hidden, BF16))
    if not turn:
        out_shape += [jax.ShapeDtypeStruct(w.shape, w.dtype) for w in weights]
        scratch.append(pltpu.SemaphoreType.DMA((2 * PARTS,)))

    def body(*refs):
        forward_kernel(keep_up, keep_down, turn, last, loss_scale, *refs)

    return pl.pallas_call(
        body,
        out_shape=out_shape,
        in_specs=in_specs,
        out_specs=[VMEM] * len(out_shape),
        scratch_shapes=scratch,
        compiler_params=pltpu.CompilerParams(vmem_limit_bytes=LIMIT if turn else 31 << 20),
        cost_estimate=pl.CostEstimate(
            flops=4 * rows * weights[0].size, bytes_accessed=4 * features, transcendentals=0
        ),
        name=f"forward_{turn}",
    )(*operands)


def contract_last(left, right):
    return lax.dot_general(left, right, (((1,), (1,)), ((), ())), preferred_element_type=F32)


def backward_kernel(
    keep_up, keep_down, turn, first_turn, up_index, down_index, *refs
):
    if first_turn:
        cot_ref, x_ref, s_ref, slope_ref, uw_ref, dw_ref, out_ref, grad_hidden, grad_normed = refs
    else:
        section, arrived_ref, held_ref, *refs = refs
        x_ref, s_ref, slope_ref, uw_ref, dw_ref, out_ref, cot_ref, grad_hidden, grad_normed = refs
        pick(section[0] == turn, arrived_ref, held_ref, cot_ref)
    size = grad_hidden.shape[-1]
    width_blocks = grad_normed.shape[0]
    hidden_blocks = grad_hidden.shape[0]
    grad_hidden[...] = jnp.zeros_like(grad_hidden)
    grad_normed[...] = jnp.zeros_like(grad_normed)
    group = DOWN_GROUP

    def down_step(step, carry):
        for ee in range(DOWN_UNROLL):
            e = step * DOWN_UNROLL + ee
            left = cot_ref[:, lane_block(e, size)]
            for k in range(0, keep_down, group):
                first = pl.multiple_of((e * keep_down + k) * size, group * size)
                term = contract_last(left, dw_ref[pl.ds(first, group * size), :])
                for q in range(group):
                    h = down_index[e * keep_down + k + q]
                    grad_hidden[h] += term[:, q * size : (q + 1) * size]
        return carry

    lax.fori_loop(0, width_blocks // DOWN_UNROLL, down_step, 0)
    part = UP_GROUP

    def up_step(step, carry):
        for cc in range(UP_UNROLL):
            c = step * UP_UNROLL + cc
            left = (slope_ref[c] * grad_hidden[c]).astype(BF16)
            for k in range(0, keep_up, part):
                first = pl.multiple_of((c * keep_up + k) * size, part * size)
                term = contract_last(left, uw_ref[pl.ds(first, part * size), :])
                for q in range(part):
                    w = up_index[c * keep_up + k + q]
                    grad_normed[w] += term[:, q * size : (q + 1) * size]
        return carry

    lax.fori_loop(0, hidden_blocks // UP_UNROLL, up_step, 0)
    x = x_ref[...].astype(F32)
    features = x.shape[1]
    inverse = lax.rsqrt(jnp.mean(x * x, axis=-1, keepdims=True) + EPSILON)
    along = jnp.zeros((x.shape[0], size), F32)
    for b in range(width_blocks):
        cols = slice(b * size, (b + 1) * size)
        scaled = grad_normed[b] * s_ref[:, cols]
        grad_normed[b] = scaled
        along += scaled * x_ref[:, cols].astype(F32)
    mean = jnp.sum(along, axis=-1, keepdims=True) * (1.0 / features)
    factor = inverse * inverse * inverse * mean
    for b in range(width_blocks):
        cols = slice(b * size, (b + 1) * size)
        grad = inverse * grad_normed[b] - x_ref[:, cols].astype(F32) * factor
        out_ref[:, cols] = (cot_ref[:, cols].astype(F32) + grad).astype(BF16)


def section_backward(turn, first_turn, states, stream, scale_plus, slope, weights, indices):
    rows, features = stream.shape
    size = weights[0].shape[1]
    hidden_blocks, keep_up = indices[0].shape
    width_blocks, keep_down = indices[1].shape

    def body(*refs):
        backward_kernel(keep_up, keep_down, turn, first_turn, *refs)

    result = jax.ShapeDtypeStruct((rows, features), BF16)
    out_shape = [result] if first_turn else [result, result]
    in_specs = [SMEM, SMEM] + ([VMEM] if first_turn else [SMEM, VMEM, VMEM]) + [VMEM] * 5
    return pl.pallas_call(
        body,
        out_shape=out_shape,
        in_specs=in_specs,
        out_specs=[VMEM] * len(out_shape),
        scratch_shapes=[
            pltpu.VMEM((hidden_blocks, rows, size), F32),
            pltpu.VMEM((width_blocks, rows, size), F32),
        ],
        compiler_params=pltpu.CompilerParams(vmem_limit_bytes=LIMIT),
        cost_estimate=pl.CostEstimate(
            flops=30000000000 if turn == 1 else 1000000, bytes_accessed=100000, transcendentals=0
        ),
        name=f"backward_{turn}",
    )(*[index.reshape(-1) for index in indices], *states, stream, scale_plus, slope, *weights)


def join_kernel(own_ref, after_ref, before_ref, low_ref, high_ref, out_ref):
    rows = own_ref.shape[-1]
    half = low_ref.shape[0]

    def step(h, carry):
        for first, far_ref in ((0, low_ref), (half, high_ref)):
            at = first + h
            for i, piece in enumerate((own_ref[at], after_ref[at], before_ref[at], far_ref[h])):
                out_ref[at, :, i * rows : (i + 1) * rows] = piece
        return carry

    lax.fori_loop(0, half, step, 0)


def join_pieces(pieces):
    blocks, size, rows = pieces[0].shape
    return pl.pallas_call(
        join_kernel,
        out_shape=jax.ShapeDtypeStruct((blocks, size, ROWS * rows), pieces[0].dtype),
        in_specs=[VMEM] * len(pieces),
        out_specs=VMEM,
        compiler_params=pltpu.CompilerParams(vmem_limit_bytes=LIMIT),
        cost_estimate=pl.CostEstimate(
            flops=1000000, bytes_accessed=8 * pieces[0].size, transcendentals=0
        ),
        name="join_pieces",
    )(*pieces)


def weight_kernel(keep_down, columns, place, down_index, *refs):
    joined_ref, cot_ref, keep_ref, give_ref, block_sum, largest = refs
    size = cot_ref.shape[1] // columns
    chunk = block_sum.shape[0] // CORES
    blocks = block_sum.shape[0] // size
    far = pl.program_id(0)
    y, z, core = place[0], place[1], place[2]
    chips = pl.num_programs(0)
    owner = y * chips + lax.rem(z + place[3 + far], chips)

    @pl.when(far == 0)
    def _():
        largest[...] = jnp.zeros_like(largest)

    top = largest[...]
    for g in range(blocks):
        b = owner * blocks + g
        e = lax.div(b, keep_down) - y * columns
        h = down_index[b]
        term = jnp.dot(joined_ref[h], cot_ref[:, lane_block(e, size)], preferred_element_type=F32)
        block_sum[g * size : (g + 1) * size, :] = term
        top = jnp.maximum(top, jnp.max(jnp.abs(term).reshape(-1, 8, size), axis=0))
    largest[...] = top
    rows = pl.ds(pl.multiple_of(far * chunk, 8), chunk)
    keep_ref[rows, :] = block_sum[pl.ds(pl.multiple_of(core * chunk, 8), chunk), :]
    give_ref[rows, :] = block_sum[pl.ds(pl.multiple_of((1 - core) * chunk, 8), chunk), :]

    @pl.when(far == chips - 1)
    def _():
        peak = jnp.broadcast_to(jnp.max(top), (8, size))
        keep_ref[chips * chunk :, :] = peak
        give_ref[chips * chunk :, :] = peak


def weight_gradient(joined, cot, down_index, place, chips, owners):
    size = joined.shape[1]
    width_blocks, keep_down = down_index.shape
    columns = cot.shape[1] // size
    total_rows = width_blocks * keep_down * size
    chunk = split_range(total_rows, owners)

    def body(*refs):
        weight_kernel(keep_down, columns, *refs)

    shape = jax.ShapeDtypeStruct((chips * chunk + 8, size), F32)
    return pl.pallas_call(
        body,
        out_shape=[shape, shape],
        grid_spec=pltpu.PrefetchScalarGridSpec(
            num_scalar_prefetch=2,
            grid=(chips,),
            in_specs=[
                pl.BlockSpec(joined.shape, lambda i, *_: (0, 0, 0), pipeline_mode=pl.Buffered(1)),
                pl.BlockSpec(cot.shape, whole),
            ],
            out_specs=[pl.BlockSpec(shape.shape, whole)] * 2,
            scratch_shapes=[
                pltpu.VMEM((CORES * chunk, size), F32),
                pltpu.VMEM((8, size), F32),
            ],
        ),
        compiler_params=pltpu.CompilerParams(
            dimension_semantics=("arbitrary",), vmem_limit_bytes=40 << 20
        ),
        cost_estimate=pl.CostEstimate(
            flops=2 * cot.shape[0] * chips * CORES * chunk * size,
            bytes_accessed=2 * joined.size,
            transcendentals=0,
        ),
        name="weight_gradient",
    )(place, down_index.reshape(-1), joined, cot)


def dp_route(rows, chips, move):
    owners = rows * chips * CORES
    route = []
    for source in range(owners):
        y, rest = divmod(source, chips * CORES)
        z, core = divmod(rest, CORES)
        y, z, core = move(y, z, core)
        route.append((source, (y % rows * chips + z % chips) * CORES + core % CORES))
    return route


def hidden_pieces(turned, rows, chips):
    assert rows == ROWS and chips == CHIPS == len(ORDER)
    half = turned.shape[0] // 2
    down = dp_route(rows, chips, lambda y, z, core: (y - 1, z, core))
    up = dp_route(rows, chips, lambda y, z, core: (y + 1, z, core))
    after = lax.ppermute(turned, "dp", down)
    before = lax.ppermute(turned, "dp", up)
    low = lax.ppermute(after[:half], "dp", down)
    high = lax.ppermute(before[half:], "dp", up)
    return [turned, after, before, low, high]


def dp_place(rows, chips, columns):
    number = lax.axis_index("dp")
    y = lax.div(number, chips * CORES)
    z = lax.rem(lax.div(number, CORES), chips)
    place = jnp.stack([y, z, lax.rem(number, CORES)] + [jnp.int32(far) for far in ORDER])
    firsts = [lax.rem(y + rows - r, rows) * columns for r in range(rows)]
    return place, firsts


def reduce_weight_gradient(joined, cot, down_index, place, firsts, rows, chips):
    owners = rows * chips * CORES
    columns = split_range(cot.shape[1], rows)
    received = []
    for r in (0, 1, rows - 1, 2):
        part = lax.dynamic_slice_in_dim(cot, firsts[r], columns, 1)
        if r:
            route = dp_route(rows, chips, lambda y, z, core: (y - r, z, core))
            part = lax.ppermute(part, "dp", route)
        received.append(part)
    keep, give = weight_gradient(
        joined, jnp.concatenate(received, axis=0), down_index, place, chips, owners
    )
    swap = dp_route(rows, chips, lambda y, z, core: (y, z, core + 1))
    total = keep + lax.ppermute(give, "dp", swap)
    chunk = split_range(keep.shape[0] - 8, chips)
    bound = jnp.maximum(total[chips * chunk : chips * chunk + 1], 1e-30)
    power = jnp.floor(13.0 - jnp.log2(bound))

    def send(values, power, steps):
        tag = jnp.broadcast_to(power, (TAG, power.shape[1]))
        coded = jnp.concatenate([values * jnp.exp2(power), tag], axis=0).astype(F16)
        route = dp_route(rows, chips, lambda y, z, core: (y, z + steps, core))
        got = lax.ppermute(coded, "dp", route).astype(F32)
        power = got[-TAG : 1 - TAG]
        return got[:-TAG] * jnp.exp2(-power), power

    half = chunk // 2
    middle = 5 * chunk
    from_below, power_below = send(total[chunk : 3 * chunk], power, 1)
    from_above, power_above = send(total[3 * chunk : middle], power, -1)
    low, power_low = send(total[middle : middle + half], power, 2)
    high, power_high = send(total[middle + half : middle + chunk], power, -2)
    upward = total[6 * chunk : 7 * chunk] + from_below[chunk:]
    upward = jnp.concatenate([upward[:half] + low, upward[half:]], axis=0)
    downward = total[7 * chunk : 8 * chunk] + from_above[chunk:]
    downward = jnp.concatenate([downward[:half], downward[half:] + high], axis=0)
    up_power = jnp.minimum(jnp.minimum(power, power_below), power_low) - 2.0
    down_power = jnp.minimum(jnp.minimum(power, power_above), power_high) - 2.0
    result = total[:chunk] + from_below[:chunk] + from_above[:chunk]
    result = result + send(upward, up_power, 2)[0]
    return result + send(downward, down_power, -2)[0]


def lookup(step_values, table):
    rows = step_values.shape[0]
    result = jnp.broadcast_to(table[0][None, :], (rows, table.shape[1]))
    for i in range(1, table.shape[0]):
        result = jnp.where((step_values == i)[:, None], table[i][None, :], result)
    return result


def per_device(
    clean_latent,
    noise_latent,
    teacher_velocity,
    step_index,
    modulation,
    up_weight,
    up_rows,
    down_weight,
    down_rows,
):
    section_count = lax.axis_size("section")
    section_number = lax.axis_index("section")
    owner_count = lax.axis_size("dp")
    row_total, feature_count = clean_latent.shape
    size = up_weight.shape[2]
    loss_scale = 1.0 / math.sqrt(row_total * owner_count)
    up_flat = lax.all_gather(up_weight, "dp", axis=1, tiled=True)[0]
    up_index = up_rows[0]
    down_flat = down_weight[0]
    down_index = down_rows[0]
    table = modulation[0]
    fraction = (step_index.astype(F32) + 1.0) / table.shape[0]
    entry = (
        (1.0 - fraction)[:, None] * clean_latent.astype(F32)
        + fraction[:, None] * noise_latent.astype(F32)
    ).astype(BF16)
    scale_plus = 1.0 + lookup(step_index, table)
    indices = (up_index, down_index)
    section = section_number.reshape(1).astype(jnp.int32)
    rows = split_range(owner_count, CHIPS * CORES)
    place, firsts = dp_place(rows, CHIPS, split_range(feature_count, rows))
    opening = section_number == 0
    section, entry, place, firsts, opening = lax.optimization_barrier(
        (section, entry, place, firsts, opening)
    )

    result, *weights = section_forward(
        0, False, loss_scale, (entry,), scale_plus, (up_flat, down_flat), indices, None
    )
    mine = entry
    for turn in range(1, section_count):
        last = turn == section_count - 1
        arrived = lax.ppermute(result, "section", [(turn - 1, turn)])
        result, mine, *kept = section_forward(
            turn, last, loss_scale, (section, arrived, mine), scale_plus, weights, indices,
            teacher_velocity,
        )
    slope, turned = kept
    cotangent = result
    pieces = hidden_pieces(turned, rows, CHIPS)
    states = (cotangent,)
    for turn in range(section_count - 1, 0, -1):
        first_turn = turn == section_count - 1
        sent, *moved = section_backward(
            turn, first_turn, states, mine, scale_plus, slope, weights, indices
        )
        if not first_turn:
            (cotangent,) = moved
        arrived = lax.ppermute(sent, "section", [(turn, turn - 1)])
        states = (section, arrived, cotangent)
    joined, arrived = lax.optimization_barrier((join_pieces(pieces), arrived))
    cotangent = jnp.where(opening, arrived, cotangent)

    return reduce_weight_gradient(joined, cotangent, down_index, place, firsts, rows, CHIPS)[None]


def solution(mesh):
    in_specs = (
        P("dp", None),
        P("dp", None),
        P("dp", None),
        P("dp"),
        P("section", None, None),
        P("section", "dp", None),
        P("section", None, None),
        P("section", None, None),
        P("section", None, None),
    )
    out_specs = P("section", "dp", None)
    return jax.shard_map(
        per_device, mesh=mesh, in_specs=in_specs, out_specs=out_specs, check_vma=False
    )
```

```python
import math

import jax
import jax.numpy as jnp
from jax import lax
from jax.experimental import pallas as pl
from jax.experimental.pallas import tpu as pltpu
from jax.sharding import PartitionSpec as P

EPSILON = 1e-06
F32 = jnp.float32
BF16 = jnp.bfloat16
F16 = jnp.float16
CORES = 2
CHIPS = 8
ORDER = (0, 1, 3, 7, 5, 4, 2, 6)
TAG = 16
FORWARD_GROUP = 4
DOWN_GROUP = 12
UP_GROUP = 6
UP_UNROLL = 16
DOWN_UNROLL = 3
FORWARD_UNROLL = 8
FORWARD_DOWN = 3
LIMIT = 12 << 20
PARTS = 4
ROWS = 4
GELU_A = math.sqrt(2.0 / math.pi)
GELU_B = 0.044715


def lane_block(index, size):
    return pl.ds(pl.multiple_of(index * size, size), size)


def split_range(total, parts):
    assert total % parts == 0
    return total // parts


def gelu_parts(v):
    squared = v * v
    t = jnp.tanh(v * (GELU_A + (GELU_A * GELU_B) * squared))
    half = 0.5 * (1.0 + t)
    slope = half + (0.5 * v) * (1.0 - t * t) * (GELU_A + (3.0 * GELU_A * GELU_B) * squared)
    return v * half, slope


def pick(take, arrived_ref, held_ref, out_ref):
    @pl.when(take)
    def _():
        out_ref[...] = arrived_ref[...]

    @pl.when(jnp.logical_not(take))
    def _():
        out_ref[...] = held_ref[...]


def part_copy(source, target, part, semaphore):
    rows = source.shape[0] // PARTS
    first = part * rows
    span = pl.ds(first if isinstance(part, int) else pl.multiple_of(first, rows), rows)
    return pltpu.make_async_copy(source.at[span, :], target.at[span, :], semaphore)


def forward_kernel(keep_up, keep_down, turn, last, loss_scale, *refs):
    refs = list(refs)
    up_index, down_index = refs[:2]
    del refs[:2]
    if turn:
        section, arrived_ref, held_ref = refs[:3]
        del refs[:3]
    else:
        x_ref = refs.pop(0)
    s_ref, uw_ref, dw_ref = refs[:3]
    del refs[:3]
    if last:
        teacher_ref = refs.pop(0)
    out_ref = refs.pop(0)
    if turn:
        x_ref = refs.pop(0)
        pick(section[0] == turn, arrived_ref, held_ref, x_ref)
    if last:
        slope_ref, turned_ref, normed, hidden = refs
    elif turn:
        normed, hidden = refs
    else:
        uw_to, dw_to, normed, hidden, arrival = refs
        uw_from, dw_from = uw_ref, dw_ref
        uw_ref, dw_ref = uw_to, dw_to

    def up_copy(part):
        return part_copy(uw_from, uw_to, part, arrival.at[part])

    def down_copy(part):
        return part_copy(dw_from, dw_to, part, arrival.at[PARTS + part])

    if not turn:
        for part in range(PARTS):
            up_copy(part).start()
    size = normed.shape[-1]
    width_blocks = normed.shape[0]
    hidden_blocks = hidden.shape[0]
    x = x_ref[...].astype(F32)
    inverse = lax.rsqrt(jnp.mean(x * x, axis=-1, keepdims=True) + EPSILON)
    for b in range(width_blocks):
        cols = slice(b * size, (b + 1) * size)
        piece = x_ref[:, cols].astype(F32)
        normed[b] = (piece * inverse * s_ref[:, cols]).astype(BF16)

    rows = keep_up * size
    up_unroll, down_unroll = FORWARD_UNROLL, FORWARD_DOWN
    if not turn:
        up_unroll, down_unroll = hidden_blocks // PARTS, width_blocks // PARTS

    def up_step(step, carry):
        if not turn:
            up_copy(step).wait()
            down_copy(step).start()
        for cc in range(up_unroll):
            c = step * up_unroll + cc
            left = jnp.concatenate(
                [normed[up_index[c * keep_up + k]] for k in range(keep_up)], axis=1
            )
            first = pl.multiple_of(c * rows, rows)
            pre = jnp.dot(left, uw_ref[pl.ds(first, rows), :], preferred_element_type=F32)
            act, slope = gelu_parts(pre)
            act = act.astype(BF16)
            hidden[c] = act
            if last:
                slope_ref[c] = slope
                turned_ref[c] = act.T
        return carry

    group = FORWARD_GROUP

    def down_step(step, carry):
        if not turn:
            down_copy(step).wait()
        for ee in range(down_unroll):
            e = step * down_unroll + ee
            acc = x_ref[:, lane_block(e, size)].astype(F32)
            for k in range(0, keep_down, group):
                left = jnp.concatenate(
                    [hidden[down_index[e * keep_down + k + q]] for q in range(group)], axis=1
                )
                first = pl.multiple_of((e * keep_down + k) * size, group * size)
                acc = acc + jnp.dot(
                    left, dw_ref[pl.ds(first, group * size), :], preferred_element_type=F32
                )
            result = acc.astype(BF16)
            if last:
                target = teacher_ref[:, lane_block(e, size)].astype(F32)
                result = ((result.astype(F32) - target) * loss_scale).astype(BF16)
            out_ref[:, lane_block(e, size)] = result
        return carry

    lax.fori_loop(0, hidden_blocks // up_unroll, up_step, 0)
    lax.fori_loop(0, width_blocks // down_unroll, down_step, 0)


def whole(i, *_):
    return (0, 0)


SMEM = pl.BlockSpec(memory_space=pltpu.SMEM)
VMEM = pl.BlockSpec(memory_space=pltpu.VMEM)


def section_forward(turn, last, loss_scale, states, scale_plus, weights, indices, teacher):
    rows, features = scale_plus.shape
    size = weights[0].shape[1]
    hidden_blocks, keep_up = indices[0].shape
    width_blocks, keep_down = indices[1].shape
    stream = jax.ShapeDtypeStruct((rows, features), BF16)
    out_shape = [stream]
    scratch = [pltpu.VMEM((width_blocks, rows, size), BF16)]
    hidden = (hidden_blocks, rows, size)
    operands = [index.reshape(-1) for index in indices] + list(states)
    operands += [scale_plus, *weights]
    in_specs = [SMEM, SMEM] + ([SMEM, VMEM, VMEM] if turn else [VMEM]) + [VMEM]
    in_specs += [VMEM, VMEM] if turn else [pl.BlockSpec(memory_space=pltpu.HBM)] * 2
    if last:
        operands.append(teacher)
        in_specs.append(VMEM)
    if turn:
        out_shape.append(stream)
    if last:
        turned = (hidden_blocks, size, rows)
        out_shape += [jax.ShapeDtypeStruct(hidden, F32), jax.ShapeDtypeStruct(turned, BF16)]
    scratch.append(pltpu.VMEM(hidden, BF16))
    if not turn:
        out_shape += [jax.ShapeDtypeStruct(w.shape, w.dtype) for w in weights]
        scratch.append(pltpu.SemaphoreType.DMA((2 * PARTS,)))

    def body(*refs):
        forward_kernel(keep_up, keep_down, turn, last, loss_scale, *refs)

    return pl.pallas_call(
        body,
        out_shape=out_shape,
        in_specs=in_specs,
        out_specs=[VMEM] * len(out_shape),
        scratch_shapes=scratch,
        compiler_params=pltpu.CompilerParams(vmem_limit_bytes=LIMIT if turn else 31 << 20),
        cost_estimate=pl.CostEstimate(
            flops=4 * rows * weights[0].size, bytes_accessed=4 * features, transcendentals=0
        ),
        name=f"forward_{turn}",
    )(*operands)


def contract_last(left, right):
    return lax.dot_general(left, right, (((1,), (1,)), ((), ())), preferred_element_type=F32)


def backward_kernel(
    keep_up, keep_down, turn, first_turn, up_index, down_index, *refs
):
    if first_turn:
        cot_ref, x_ref, s_ref, slope_ref, uw_ref, dw_ref, out_ref, grad_hidden, grad_normed = refs
    else:
        section, arrived_ref, held_ref, *refs = refs
        x_ref, s_ref, slope_ref, uw_ref, dw_ref, out_ref, cot_ref, grad_hidden, grad_normed = refs
        pick(section[0] == turn, arrived_ref, held_ref, cot_ref)
    size = grad_hidden.shape[-1]
    width_blocks = grad_normed.shape[0]
    hidden_blocks = grad_hidden.shape[0]
    grad_hidden[...] = jnp.zeros_like(grad_hidden)
    grad_normed[...] = jnp.zeros_like(grad_normed)
    group = DOWN_GROUP

    def down_step(step, carry):
        for ee in range(DOWN_UNROLL):
            e = step * DOWN_UNROLL + ee
            left = cot_ref[:, lane_block(e, size)]
            for k in range(0, keep_down, group):
                first = pl.multiple_of((e * keep_down + k) * size, group * size)
                term = contract_last(left, dw_ref[pl.ds(first, group * size), :])
                for q in range(group):
                    h = down_index[e * keep_down + k + q]
                    grad_hidden[h] += term[:, q * size : (q + 1) * size]
        return carry

    lax.fori_loop(0, width_blocks // DOWN_UNROLL, down_step, 0)
    part = UP_GROUP

    def up_step(step, carry):
        for cc in range(UP_UNROLL):
            c = step * UP_UNROLL + cc
            left = (slope_ref[c] * grad_hidden[c]).astype(BF16)
            for k in range(0, keep_up, part):
                first = pl.multiple_of((c * keep_up + k) * size, part * size)
                term = contract_last(left, uw_ref[pl.ds(first, part * size), :])
                for q in range(part):
                    w = up_index[c * keep_up + k + q]
                    grad_normed[w] += term[:, q * size : (q + 1) * size]
        return carry

    lax.fori_loop(0, hidden_blocks // UP_UNROLL, up_step, 0)
    x = x_ref[...].astype(F32)
    features = x.shape[1]
    inverse = lax.rsqrt(jnp.mean(x * x, axis=-1, keepdims=True) + EPSILON)
    along = jnp.zeros((x.shape[0], size), F32)
    for b in range(width_blocks):
        cols = slice(b * size, (b + 1) * size)
        scaled = grad_normed[b] * s_ref[:, cols]
        grad_normed[b] = scaled
        along += scaled * x_ref[:, cols].astype(F32)
    mean = jnp.sum(along, axis=-1, keepdims=True) * (1.0 / features)
    factor = inverse * inverse * inverse * mean
    for b in range(width_blocks):
        cols = slice(b * size, (b + 1) * size)
        grad = inverse * grad_normed[b] - x_ref[:, cols].astype(F32) * factor
        out_ref[:, cols] = (cot_ref[:, cols].astype(F32) + grad).astype(BF16)


def section_backward(turn, first_turn, states, stream, scale_plus, slope, weights, indices):
    rows, features = stream.shape
    size = weights[0].shape[1]
    hidden_blocks, keep_up = indices[0].shape
    width_blocks, keep_down = indices[1].shape

    def body(*refs):
        backward_kernel(keep_up, keep_down, turn, first_turn, *refs)

    result = jax.ShapeDtypeStruct((rows, features), BF16)
    out_shape = [result] if first_turn else [result, result]
    in_specs = [SMEM, SMEM] + ([VMEM] if first_turn else [SMEM, VMEM, VMEM]) + [VMEM] * 5
    return pl.pallas_call(
        body,
        out_shape=out_shape,
        in_specs=in_specs,
        out_specs=[VMEM] * len(out_shape),
        scratch_shapes=[
            pltpu.VMEM((hidden_blocks, rows, size), F32),
            pltpu.VMEM((width_blocks, rows, size), F32),
        ],
        compiler_params=pltpu.CompilerParams(vmem_limit_bytes=LIMIT),
        cost_estimate=pl.CostEstimate(
            flops=30000000000 if turn == 1 else 1000000, bytes_accessed=100000, transcendentals=0
        ),
        name=f"backward_{turn}",
    )(*[index.reshape(-1) for index in indices], *states, stream, scale_plus, slope, *weights)


def join_kernel(own_ref, after_ref, before_ref, low_ref, high_ref, out_ref):
    rows = own_ref.shape[-1]
    half = low_ref.shape[0]

    def step(h, carry):
        for first, far_ref in ((0, low_ref), (half, high_ref)):
            at = first + h
            for i, piece in enumerate((own_ref[at], after_ref[at], before_ref[at], far_ref[h])):
                out_ref[at, :, i * rows : (i + 1) * rows] = piece
        return carry

    lax.fori_loop(0, half, step, 0)


def join_pieces(pieces):
    blocks, size, rows = pieces[0].shape
    return pl.pallas_call(
        join_kernel,
        out_shape=jax.ShapeDtypeStruct((blocks, size, ROWS * rows), pieces[0].dtype),
        in_specs=[VMEM] * len(pieces),
        out_specs=VMEM,
        compiler_params=pltpu.CompilerParams(vmem_limit_bytes=LIMIT),
        cost_estimate=pl.CostEstimate(
            flops=1000000, bytes_accessed=8 * pieces[0].size, transcendentals=0
        ),
        name="join_pieces",
    )(*pieces)


def weight_kernel(keep_down, columns, place, down_index, *refs):
    joined_ref, cot_ref, keep_ref, give_ref, block_sum, largest = refs
    size = cot_ref.shape[1] // columns
    chunk = block_sum.shape[0] // CORES
    blocks = block_sum.shape[0] // size
    far = pl.program_id(0)
    y, z, core = place[0], place[1], place[2]
    chips = pl.num_programs(0)
    owner = y * chips + lax.rem(z + place[3 + far], chips)

    @pl.when(far == 0)
    def _():
        largest[...] = jnp.zeros_like(largest)

    top = largest[...]
    for g in range(blocks):
        b = owner * blocks + g
        e = lax.div(b, keep_down) - y * columns
        h = down_index[b]
        term = jnp.dot(joined_ref[h], cot_ref[:, lane_block(e, size)], preferred_element_type=F32)
        block_sum[g * size : (g + 1) * size, :] = term
        top = jnp.maximum(top, jnp.max(jnp.abs(term).reshape(-1, 8, size), axis=0))
    largest[...] = top
    rows = pl.ds(pl.multiple_of(far * chunk, 8), chunk)
    keep_ref[rows, :] = block_sum[pl.ds(pl.multiple_of(core * chunk, 8), chunk), :]
    give_ref[rows, :] = block_sum[pl.ds(pl.multiple_of((1 - core) * chunk, 8), chunk), :]

    @pl.when(far == chips - 1)
    def _():
        peak = jnp.broadcast_to(jnp.max(top), (8, size))
        keep_ref[chips * chunk :, :] = peak
        give_ref[chips * chunk :, :] = peak


def weight_gradient(joined, cot, down_index, place, chips, owners):
    size = joined.shape[1]
    width_blocks, keep_down = down_index.shape
    columns = cot.shape[1] // size
    total_rows = width_blocks * keep_down * size
    chunk = split_range(total_rows, owners)

    def body(*refs):
        weight_kernel(keep_down, columns, *refs)

    shape = jax.ShapeDtypeStruct((chips * chunk + 8, size), F32)
    return pl.pallas_call(
        body,
        out_shape=[shape, shape],
        grid_spec=pltpu.PrefetchScalarGridSpec(
            num_scalar_prefetch=2,
            grid=(chips,),
            in_specs=[
                pl.BlockSpec(joined.shape, lambda i, *_: (0, 0, 0), pipeline_mode=pl.Buffered(1)),
                pl.BlockSpec(cot.shape, whole),
            ],
            out_specs=[pl.BlockSpec(shape.shape, whole)] * 2,
            scratch_shapes=[
                pltpu.VMEM((CORES * chunk, size), F32),
                pltpu.VMEM((8, size), F32),
            ],
        ),
        compiler_params=pltpu.CompilerParams(
            dimension_semantics=("arbitrary",), vmem_limit_bytes=40 << 20
        ),
        cost_estimate=pl.CostEstimate(
            flops=2 * cot.shape[0] * chips * CORES * chunk * size,
            bytes_accessed=2 * joined.size,
            transcendentals=0,
        ),
        name="weight_gradient",
    )(place, down_index.reshape(-1), joined, cot)


def dp_route(rows, chips, move):
    owners = rows * chips * CORES
    route = []
    for source in range(owners):
        y, rest = divmod(source, chips * CORES)
        z, core = divmod(rest, CORES)
        y, z, core = move(y, z, core)
        route.append((source, (y % rows * chips + z % chips) * CORES + core % CORES))
    return route


def hidden_pieces(turned, rows, chips):
    assert rows == ROWS and chips == CHIPS == len(ORDER)
    half = turned.shape[0] // 2
    down = dp_route(rows, chips, lambda y, z, core: (y - 1, z, core))
    up = dp_route(rows, chips, lambda y, z, core: (y + 1, z, core))
    after = lax.ppermute(turned, "dp", down)
    before = lax.ppermute(turned, "dp", up)
    low = lax.ppermute(after[:half], "dp", down)
    high = lax.ppermute(before[half:], "dp", up)
    return [turned, after, before, low, high]


def dp_place(rows, chips, columns):
    number = lax.axis_index("dp")
    y = lax.div(number, chips * CORES)
    z = lax.rem(lax.div(number, CORES), chips)
    place = jnp.stack([y, z, lax.rem(number, CORES)] + [jnp.int32(far) for far in ORDER])
    firsts = [lax.rem(y + rows - r, rows) * columns for r in range(rows)]
    return place, firsts


def reduce_weight_gradient(joined, cot, down_index, place, firsts, rows, chips):
    owners = rows * chips * CORES
    columns = split_range(cot.shape[1], rows)
    received = []
    for r in (0, 1, rows - 1, 2):
        part = lax.dynamic_slice_in_dim(cot, firsts[r], columns, 1)
        if r:
            route = dp_route(rows, chips, lambda y, z, core: (y - r, z, core))
            part = lax.ppermute(part, "dp", route)
        received.append(part)
    keep, give = weight_gradient(
        joined, jnp.concatenate(received, axis=0), down_index, place, chips, owners
    )
    swap = dp_route(rows, chips, lambda y, z, core: (y, z, core + 1))
    total = keep + lax.ppermute(give, "dp", swap)
    chunk = split_range(keep.shape[0] - 8, chips)
    bound = jnp.maximum(total[chips * chunk : chips * chunk + 1], 1e-30)
    power = jnp.floor(13.0 - jnp.log2(bound))

    def send(values, power, steps):
        tag = jnp.broadcast_to(power, (TAG, power.shape[1]))
        coded = jnp.concatenate([values * jnp.exp2(power), tag], axis=0).astype(F16)
        route = dp_route(rows, chips, lambda y, z, core: (y, z + steps, core))
        got = lax.ppermute(coded, "dp", route).astype(F32)
        power = got[-TAG : 1 - TAG]
        return got[:-TAG] * jnp.exp2(-power), power

    half = chunk // 2
    middle = 5 * chunk
    from_below, power_below = send(total[chunk : 3 * chunk], power, 1)
    from_above, power_above = send(total[3 * chunk : middle], power, -1)
    low, power_low = send(total[middle : middle + half], power, 2)
    high, power_high = send(total[middle + half : middle + chunk], power, -2)
    upward = total[6 * chunk : 7 * chunk] + from_below[chunk:]
    upward = jnp.concatenate([upward[:half] + low, upward[half:]], axis=0)
    downward = total[7 * chunk : 8 * chunk] + from_above[chunk:]
    downward = jnp.concatenate([downward[:half], downward[half:] + high], axis=0)
    up_power = jnp.minimum(jnp.minimum(power, power_below), power_low) - 2.0
    down_power = jnp.minimum(jnp.minimum(power, power_above), power_high) - 2.0
    result = total[:chunk] + from_below[:chunk] + from_above[:chunk]
    result = result + send(upward, up_power, 2)[0]
    return result + send(downward, down_power, -2)[0]


def lookup(step_values, table):
    rows = step_values.shape[0]
    result = jnp.broadcast_to(table[0][None, :], (rows, table.shape[1]))
    for i in range(1, table.shape[0]):
        result = jnp.where((step_values == i)[:, None], table[i][None, :], result)
    return result


def per_device(
    clean_latent,
    noise_latent,
    teacher_velocity,
    step_index,
    modulation,
    up_weight,
    up_rows,
    down_weight,
    down_rows,
):
    section_count = lax.axis_size("section")
    section_number = lax.axis_index("section")
    owner_count = lax.axis_size("dp")
    row_total, feature_count = clean_latent.shape
    size = up_weight.shape[2]
    loss_scale = 1.0 / math.sqrt(row_total * owner_count)
    up_flat = lax.all_gather(up_weight, "dp", axis=1, tiled=True)[0]
    up_index = up_rows[0]
    down_flat = down_weight[0]
    down_index = down_rows[0]
    table = modulation[0]
    fraction = (step_index.astype(F32) + 1.0) / table.shape[0]
    entry = (
        (1.0 - fraction)[:, None] * clean_latent.astype(F32)
        + fraction[:, None] * noise_latent.astype(F32)
    ).astype(BF16)
    scale_plus = 1.0 + lookup(step_index, table)
    indices = (up_index, down_index)
    section = section_number.reshape(1).astype(jnp.int32)
    rows = split_range(owner_count, CHIPS * CORES)
    place, firsts = dp_place(rows, CHIPS, split_range(feature_count, rows))
    opening = section_number == 0
    section, entry, place, firsts, opening = lax.optimization_barrier(
        (section, entry, place, firsts, opening)
    )

    result, *weights = section_forward(
        0, False, loss_scale, (entry,), scale_plus, (up_flat, down_flat), indices, None
    )
    mine = entry
    for turn in range(1, section_count):
        last = turn == section_count - 1
        arrived = lax.ppermute(result, "section", [(turn - 1, turn)])
        result, mine, *kept = section_forward(
            turn, last, loss_scale, (section, arrived, mine), scale_plus, weights, indices,
            teacher_velocity,
        )
    slope, turned = kept
    cotangent = result
    pieces = hidden_pieces(turned, rows, CHIPS)
    states = (cotangent,)
    for turn in range(section_count - 1, 0, -1):
        first_turn = turn == section_count - 1
        sent, *moved = section_backward(
            turn, first_turn, states, mine, scale_plus, slope, weights, indices
        )
        if not first_turn:
            (cotangent,) = moved
        arrived = lax.ppermute(sent, "section", [(turn, turn - 1)])
        states = (section, arrived, cotangent)
    joined, arrived = lax.optimization_barrier((join_pieces(pieces), arrived))
    cotangent = jnp.where(opening, arrived, cotangent)

    return reduce_weight_gradient(joined, cotangent, down_index, place, firsts, rows, CHIPS)[None]


def solution(mesh):
    in_specs = (
        P("dp", None),
        P("dp", None),
        P("dp", None),
        P("dp"),
        P("section", None, None),
        P("section", "dp", None),
        P("section", None, None),
        P("section", None, None),
        P("section", None, None),
    )
    out_specs = P("section", "dp", None)
    return jax.shard_map(
        per_device, mesh=mesh, in_specs=in_specs, out_specs=out_specs, check_vma=False
    )
```
